32 devices in a mesh: slab: 8 (over z, x), cable: 4 (over y, core).
Axes of the slice: x: 2, y: 2, z: 4, core: 2. Of those that a mesh axis runs over, the one named last changes fastest.
Arguments:
- electric: float32 [3, 256, 128, 256], P(None, ('slab', 'cable')), may hold values from -6 to 6
- magnetic: float32 [3, 256, 128, 256], P(None, ('slab', 'cable')), may hold values from -6 to 6
- conductivity: float32 [256, 128, 256], P(('slab', 'cable')), may hold values from 0.02 to 0.8
- voltage: float32 [32, 32, 4096], P(None, None, ('slab', 'cable')), may hold values from -6 to 6
- current: float32 [32, 32, 4096], P(None, None, ('slab', 'cable')), may hold values from -6 to 6
- inverse_inductance: float32 [32, 32, 4096], P(None, None, ('slab', 'cable')), as said below
- inverse_capacitance: float32 [32, 32, 4096], P(None, None, ('slab', 'cable')), as said below
- tangent: float32 [3, 32, 4096], P(None, ('slab', 'cable')), may hold values from -4 to 4
- sample_cell: int32 [32, 4096], P(('slab', 'cable')), may hold values from 0 to 1023
- tube_length: int32 [4096], P(('slab', 'cable')), may hold values from 8 to 32
- junction_link: int32 [4096], P(('slab', 'cable')), may hold values from 0 to 127, as said below
Outputs:
- electric_new: float32 [3, 256, 128, 256], P(None, ('slab', 'cable'))
- magnetic_new: float32 [3, 256, 128, 256], P(None, ('slab', 'cable'))
- voltage_new: float32 [32, 32, 4096], P(None, None, ('slab', 'cable'))
- current_new: float32 [32, 32, 4096], P(None, None, ('slab', 'cable'))
The draws below stay inside these ranges and needn't reach their ends.
Inputs may be any that keep to these rules, and one draw needn't show every extreme that they name: `junction_link`: every aligned block of 128 entries holds each of its values once. `inverse_inductance`: symmetric, with off-diagonal entries summing to about as much as the diagonal. `inverse_capacitance`: symmetric, with off-diagonal entries summing to about as much as the diagonal.
All inputs are finite; a program needn't handle non-finite values.
Results may differ from the reference program's by a relative error of at most 0.0001.
Values sent between devices are 32-bit elements; how exact they have to be, the bound alone decides.
A program may use at most 128 MiB of HBM per device.

```python
import math
import jax
import jax.numpy as jnp
from jax import lax

COND = 32
SUB = 3
SEG_DEV = 1
CX = 8
NY = 128
NZ = 256
TUBE_DEV = 128
NX = 256
SEG = 32
TUBES = 4096
N_CABLE = 4


def matrix_block(subkey):
    first, second = jax.random.split(subkey)
    diagonal = jax.random.uniform(first, (COND, TUBES), jnp.float32, 0.3, 0.6)
    spread = 0.025
    coupling = jax.random.normal(second, (COND, COND, TUBES), jnp.float32) * spread
    coupling = 0.5 * (coupling + jnp.transpose(coupling, (1, 0, 2)))
    identity = jnp.eye(COND, dtype=jnp.float32)[:, :, None]
    return coupling * (1.0 - identity) + identity * diagonal[None]


def draw_inverse_inductance(key, part):
    return matrix_block(jax.random.fold_in(key, 11))


def draw_inverse_capacitance(key, part):
    return matrix_block(jax.random.fold_in(key, 23))


def draw_tube_length(key, part):
    values = jax.random.randint(jax.random.fold_in(key, 5), (TUBES,), SEG // 4, SEG + 1).astype(jnp.int32)
    return values.at[0].set(SEG).at[1].set(SEG // 4)


def one_block(subkey):
    return jax.random.permutation(subkey, TUBE_DEV)


def draw_junction_link(key, part):
    subkeys = jax.random.split(jax.random.fold_in(key, 7), TUBES // TUBE_DEV)
    return jax.vmap(one_block)(subkeys).reshape(TUBES).astype(jnp.int32)


def with_ends(values, own_key, smallest, largest):
    longest = values.shape.index(max(values.shape))
    spots = []
    for shift in (0, 1):
        where = [jax.random.randint(jax.random.fold_in(own_key, axis), (), 0, length) for axis, length in enumerate(values.shape)]
        where[longest] = (where[longest] + shift) % values.shape[longest]
        spots.append(tuple(where))
    return values.at[spots[0]].set(smallest).at[spots[1]].set(largest)


def steps_of(rng, dims, cuts, low, top_value):
    def one(dim, shards_of):
        heights = jax.random.uniform(jax.random.fold_in(jax.random.fold_in(rng, 6), dim), (shards_of,), jnp.float32, low / len(cuts), top_value / len(cuts))
        return jnp.repeat(jnp.exp(heights), dims[dim] // shards_of).reshape((-1,) + (1,) * (len(dims) - dim - 1))

    level = one(*cuts[0])
    for cut in cuts[1:]:
        level = level * one(*cut)
    return level


def scatter_about(own_key, shape, deviation, most, pieces=(), held_as=jnp.bfloat16):
    array = jax.random.normal(own_key, shape, jnp.float32) * deviation
    if len(pieces) > 0:
        array = steps_of(own_key, shape, pieces, -0.22, 0.18) * array
    return jnp.clip(array, min=-most, max=most).astype(held_as)


def setup_inputs(seed: int = 0) -> dict:
    key_list = jax.random.split(jax.random.key(seed), 12)
    return {
        "electric": scatter_about(key_list[0], (3, NX, NY, NZ), 1.0, 6.0, ((1, 32),), jnp.float32),
        "magnetic": scatter_about(key_list[1], (3, NX, NY, NZ), 1.0, 6.0, ((1, 32),), jnp.float32),
        "conductivity": jnp.clip(jnp.exp(math.log(0.8) - 3.6888795 * jax.random.uniform(key_list[2], (NX, NY, NZ), jnp.float32) ** steps_of(key_list[2], (NX, NY, NZ), ((0, 32),), -0.2, 0.2)), 0.02, 0.8),
        "voltage": scatter_about(key_list[3], (COND, SEG, TUBES), 1.0, 6.0, ((2, 32),), jnp.float32),
        "current": scatter_about(key_list[4], (COND, SEG, TUBES), 1.0, 6.0, ((2, 32),), jnp.float32),
        "inverse_inductance": draw_inverse_inductance(jax.random.fold_in(key_list[11], 71), 0),
        "inverse_capacitance": draw_inverse_capacitance(jax.random.fold_in(key_list[11], 71), 0),
        "tangent": scatter_about(key_list[7], (3, SEG, TUBES), 1.0, 4.0, ((1, 32),), jnp.float32),
        "sample_cell": with_ends(jax.random.randint(key_list[8], (SEG, TUBES), 0, CX * NY), jax.random.fold_in(key_list[8], 1), 0, (CX * NY) - 1).astype(jnp.int32),
        "tube_length": draw_tube_length(jax.random.fold_in(key_list[11], 71), 0),
        "junction_link": draw_junction_link(jax.random.fold_in(key_list[11], 71), 0),
    }


courant = 0.5
highest = lax.Precision.HIGHEST


def forward_diff(quantity, along):
    extent = quantity.shape[along]
    shifted = jnp.concatenate([lax.slice_in_dim(quantity, 1, extent, axis=along), jnp.zeros_like(lax.slice_in_dim(quantity, 0, 1, axis=along))], axis=along)
    return shifted - quantity


def backward_diff(quantity, along):
    extent = quantity.shape[along]
    shifted = jnp.concatenate([jnp.zeros_like(lax.slice_in_dim(quantity, 0, 1, axis=along)), lax.slice_in_dim(quantity, 0, extent - 1, axis=along)], axis=along)
    return quantity - shifted


def reference(electric, magnetic, conductivity, voltage, current, inverse_inductance, inverse_capacitance, tangent, sample_cell, tube_length, junction_link):
    keep_factor = (1.0 - conductivity) / (1.0 + conductivity)
    curl_factor = courant / (1.0 + conductivity)
    magnetic_new = magnetic - courant * jnp.stack([
        forward_diff(electric[2], 1) - forward_diff(electric[1], 2),
        forward_diff(electric[0], 2) - forward_diff(electric[2], 0),
        forward_diff(electric[1], 0) - forward_diff(electric[0], 1)])
    segment_ids = jnp.arange(SEG, dtype=jnp.int32)
    tube_ids = jnp.arange(TUBES, dtype=jnp.int32)
    global_cell = (((segment_ids // SEG_DEV) * (CX * NY * NZ)).astype(jnp.int32)[:, None] + sample_cell * NZ + (tube_ids % NZ)[None, :]).astype(jnp.int32)
    flat_field = electric.reshape(3, -1)
    drive_field = tangent[0] * flat_field[0][global_cell] + tangent[1] * flat_field[1][global_cell] + tangent[2] * flat_field[2][global_cell]
    live = (segment_ids[:, None] < tube_length[None, :]).astype(jnp.float32)
    last_pick = (segment_ids[:, None] == (tube_length - 1)[None, :]).astype(jnp.float32)
    owner = jnp.arange(TUBES, dtype=jnp.int32) // TUBE_DEV
    feeder_owner = owner // N_CABLE * N_CABLE + (owner % N_CABLE + N_CABLE - 1) % N_CABLE
    feeder_tube = (feeder_owner * TUBE_DEV + junction_link).astype(jnp.int32)
    volts = voltage
    amps = current
    for substep in range(SUB):
        volts_next = jnp.concatenate([volts[:, 1:], jnp.zeros_like(volts[:, :1])], axis=1)
        push = volts_next - volts - drive_field[None]
        amps = live[None] * (amps - jnp.einsum('cdt,dst->cst', inverse_inductance, push, precision=highest))
        tube_end = jnp.sum(amps * last_pick[None], axis=1)
        inflow = tube_end[:, feeder_tube]
        amps_prev = jnp.concatenate([inflow[:, None], amps[:, :-1]], axis=1)
        volts = live[None] * (volts - jnp.einsum('cdt,dst->cst', inverse_capacitance, amps - amps_prev, precision=highest))
    induced = jnp.mean(amps, axis=0)
    flat_index = global_cell.reshape(-1)
    deposit = jnp.stack([jax.ops.segment_sum((tangent[component] * induced).reshape(-1), flat_index, num_segments=NX * NY * NZ) for component in range(3)]).reshape(electric.shape)
    curl_h = jnp.stack([
        backward_diff(magnetic_new[2], 1) - backward_diff(magnetic_new[1], 2),
        backward_diff(magnetic_new[0], 2) - backward_diff(magnetic_new[2], 0),
        backward_diff(magnetic_new[1], 0) - backward_diff(magnetic_new[0], 1)])
    electric_new = keep_factor[None] * electric + curl_factor[None] * (curl_h - deposit)
    return electric_new, magnetic_new, volts, amps
```

```python
import functools

import jax
import jax.numpy as jnp
from jax import lax
from jax.experimental import pallas as pl
from jax.experimental.pallas import tpu as pltpu
from jax.sharding import PartitionSpec as P

COURANT = 0.5
LANES = 128
SUBLANES = 8
AXES = ("slab", "cable")
OPENING_VMEM = 28 << 20
CLOSING_VMEM = 8 << 20


def params(*semantics):
    if semantics:
        return pltpu.CompilerParams(dimension_semantics=semantics)
    return pltpu.CompilerParams()


def whole_block(shape):
    rank = len(shape)
    return pl.BlockSpec(shape, lambda i: (0,) * rank)


def everyone(mesh_shape):
    slabs, cables = mesh_shape
    count = slabs * cables
    me = lax.axis_index("slab") * cables + lax.axis_index("cable")
    return count, me, lambda peer: (peer // cables, peer % cables)


def greet_all(count, me, place):
    barrier = pltpu.get_barrier_semaphore()

    def greet(k, carry):
        pl.semaphore_signal(
            barrier, inc=1, device_id=place((me + k) % count),
            device_id_type=pl.DeviceIdType.MESH,
        )
        return carry

    lax.fori_loop(1, count, greet, 0)
    return lambda: pl.semaphore_wait(barrier, count - 1)


def row_exchange(count, me, place, send_ref, recv_ref, send_sem, recv_sem):
    def outgoing(k):
        peer = (me + k) % count
        return pltpu.make_async_remote_copy(
            src_ref=send_ref.at[peer], dst_ref=recv_ref.at[me],
            send_sem=send_sem.at[k], recv_sem=recv_sem.at[k],
            device_id=place(peer), device_id_type=pl.DeviceIdType.MESH,
        )

    def incoming(k):
        peer = (me + count - k) % count
        return pltpu.make_async_remote_copy(
            src_ref=send_ref.at[peer], dst_ref=recv_ref.at[peer],
            send_sem=send_sem.at[k], recv_sem=recv_sem.at[k],
            device_id=place(peer), device_id_type=pl.DeviceIdType.MESH,
        )

    def start(k, carry):
        outgoing(k).start()
        return carry

    def finish(k, carry):
        outgoing(k).wait_send()
        incoming(k).wait_recv()
        return carry

    return (
        lambda: lax.fori_loop(1, count, start, 0),
        lambda: lax.fori_loop(1, count, finish, 0),
    )


def edge_copy(count, me, place, by, src, dst, send_sem, recv_sem, settle=None):
    has_target = (me + by >= 0) & (me + by < count)
    has_source = (me - by >= 0) & (me - by < count)
    target = (me + by + count) % count
    copy = pltpu.make_async_remote_copy(
        src_ref=src, dst_ref=dst, send_sem=send_sem, recv_sem=recv_sem,
        device_id=place(target), device_id_type=pl.DeviceIdType.MESH,
    )

    def start():
        @pl.when(has_target)
        def _():
            copy.start()

    def received():
        @pl.when(has_source)
        def _():
            copy.wait_recv()
            if settle is not None:
                settle()

        @pl.when(jnp.logical_not(has_source))
        def _():
            dst[...] = jnp.zeros(dst.shape, jnp.float32)

    def sent():
        @pl.when(has_target)
        def _():
            copy.wait_send()

    return start, received, sent


def magnetic_layer(field, magnetic, fresh, layer, following):
    ny = field.shape[2]
    for first in range(0, ny, SUBLANES):
        rows = pl.ds(first, SUBLANES)
        ex, ey, ez = (field[k, layer, rows, :] for k in range(3))
        if first + SUBLANES < ny:
            after = pl.ds(first + 1, SUBLANES)
            dy_ez = field[2, layer, after, :] - ez
            dy_ex = field[0, layer, after, :] - ex
        else:
            dy_ez, dy_ex = ahead(ez, 0), ahead(ex, 0)
        dx_ez = field[2, following, rows, :] - ez
        dx_ey = field[1, following, rows, :] - ey
        fresh[0, layer, rows, :] = magnetic[0, layer, rows, :] - COURANT * (dy_ez - ahead(ey, 1))
        fresh[1, layer, rows, :] = magnetic[1, layer, rows, :] - COURANT * (ahead(ex, 1) - dx_ez)
        fresh[2, layer, rows, :] = magnetic[2, layer, rows, :] - COURANT * (dx_ey - dy_ex)


def partial_edge(field, magnetic, layer, part):
    ny = field.shape[2]
    for first in range(0, ny, SUBLANES):
        rows = pl.ds(first, SUBLANES)
        ex, ey, ez = (field[k, layer, rows, :] for k in range(3))
        if first + SUBLANES < ny:
            dy_ex = field[0, layer, pl.ds(first + 1, SUBLANES), :] - ex
        else:
            dy_ex = ahead(ex, 0)
        part[0, rows, :] = magnetic[1, layer, rows, :] - COURANT * (ahead(ex, 1) + ez)
        part[1, rows, :] = magnetic[2, layer, rows, :] + COURANT * (ey + dy_ex)


def cell_codes(cell_ref, halves, depth, chunks, word_ref):
    trays = cell_ref.shape[0] // halves
    for half in range(halves):
        cells = cell_ref[pl.ds(half, trays, stride=halves), :]
        order = lax.broadcasted_iota(jnp.int32, cells.shape, 0)
        late = jnp.zeros(cells.shape, jnp.int32)
        for tray in range(trays):
            again = (cells == cells[tray : tray + 1]) & (order > tray)
            late = jnp.where(again, 1, late)
        block = jnp.where(late == 0, cells >> 3, -1)
        code = jnp.left_shift((order & (SUBLANES - 1)) | SUBLANES, (cells & (SUBLANES - 1)) * 4)

        def one(layer, carry):
            here = lax.broadcasted_iota(jnp.int32, (chunks, LANES), 0) + layer * chunks
            for group in range(trays // SUBLANES):
                word = jnp.zeros((chunks, LANES), jnp.int32)
                for tray in range(group * SUBLANES, (group + 1) * SUBLANES):
                    hit = block[tray : tray + 1] == here
                    word = word | jnp.where(hit, code[tray : tray + 1], 0)
                word_ref[half, group, layer] = word
            return carry

        lax.fori_loop(0, depth, one, 0)


def opening_kernel(
    mesh_shape, cell_hbm, tangent_hbm, electric_hbm, magnetic_hbm, conductivity_hbm,
    volts_hbm, amps_hbm, inductance_hbm, capacitance_hbm, length_hbm, link_hbm,
    cell_ref, tangent_ref, induced_out, field, fresh, sigma, below_ref, word_ref,
    volts_out, amps_out, length_ref, link_ref,
    magnetic, volts_ref, amps_ref, inductance_ref, capacitance_ref, work_ref,
    flat_ref, send_ref, recv_ref, send_back_ref, recv_back_ref, part_ref,
    drive_ref, sum_ref, ends_ref, fed_ref, last_end_ref, last_fed_ref,
    amps_shift_ref, volts_shift_ref, inflow_ref,
    load_sem, send_sem, recv_sem, send_back_sem, recv_back_sem, edge_sem, feed_sem,
):
    depth, ny, nz = magnetic.shape[1:]
    count, me, place = everyone(mesh_shape)
    pairs = [(cell_hbm, cell_ref), (tangent_hbm, tangent_ref)]
    pairs += [(electric_hbm.at[:, i], field.at[:, i]) for i in range(depth)]
    pairs += [
        (magnetic_hbm.at[:, depth - 1], magnetic.at[:, depth - 1]),
        (volts_hbm, volts_ref),
        (inductance_hbm, inductance_ref),
        (length_hbm, length_ref),
        (link_hbm, link_ref),
        (magnetic_hbm.at[:, pl.ds(0, depth - 1)], magnetic.at[:, pl.ds(0, depth - 1)]),
        (amps_hbm, amps_ref),
        (capacitance_hbm, capacitance_ref),
        (conductivity_hbm, sigma),
    ]
    loads = [
        pltpu.make_async_copy(src, dst, load_sem.at[i]) for i, (src, dst) in enumerate(pairs)
    ]
    for load in loads:
        load.start()
    greeted = greet_all(count, me, place)
    loads[0].wait()
    loads[1].wait()
    layers, top, line, lengths, links, rest, amps_load, capacitance_load, sigma_load = (
        loads[2 : 2 + depth], loads[2 + depth], loads[3 + depth : 5 + depth],
        *loads[5 + depth :],
    )

    halves = nz // LANES
    trays = cell_ref.shape[0] // halves
    groups = trays // SUBLANES
    chunks = ny // SUBLANES
    found = {}
    for layer in range(depth):
        layers[layer].wait()
        for half in range(halves):
            for group in range(groups):
                start = group * SUBLANES * halves + half
                cells = cell_ref[pl.ds(start, SUBLANES, stride=halves), :]
                low = cells & (SUBLANES - 1)
                high = (cells >> 3) - layer * chunks

                def pick(chunk, found):
                    rows = pl.ds(pl.multiple_of(chunk * SUBLANES, SUBLANES), SUBLANES)
                    hit = high == chunk
                    out = []
                    for k in range(3):
                        tile = field[k, layer, rows, half * LANES : (half + 1) * LANES]
                        value = jnp.take_along_axis(tile, low, axis=0)
                        out.append(jnp.where(hit, value, found[k]))
                    return tuple(out)

                empty = (jnp.zeros((SUBLANES, LANES), jnp.float32),) * 3
                found[half, group] = lax.fori_loop(
                    0, chunks, pick, found.get((half, group), empty), unroll=4
                )
    for half in range(halves):
        for group in range(groups):
            where = pl.ds(group * SUBLANES * halves + half, SUBLANES, stride=halves)
            x, y, z = found[half, group]
            flat_ref[where, :] = (
                tangent_ref[0, where, :] * x
                + tangent_ref[1, where, :] * y
                + tangent_ref[2, where, :] * z
            )
    for row in range(count):
        send_ref[row] = flat_ref[row : row + 1, :]
    start_rows, finish_rows = row_exchange(
        count, me, place, send_ref, recv_ref, send_sem, recv_sem
    )
    greeted()
    start_rows()

    top.wait()
    partial_edge(field, magnetic, depth - 1, part_ref)

    def complete():
        for first in range(0, ny, SUBLANES):
            rows = pl.ds(first, SUBLANES)
            below_ref[0, rows, :] = below_ref[0, rows, :] + COURANT * field[2, 0, rows, :]
            below_ref[1, rows, :] = below_ref[1, rows, :] - COURANT * field[1, 0, rows, :]

    send_above, above_here, above_sent = edge_copy(
        count, me, place, -1, field.at[pl.ds(1, 2), 0], field.at[pl.ds(1, 2), depth],
        edge_sem.at[0], edge_sem.at[1],
    )
    send_below, below_here, below_sent = edge_copy(
        count, me, place, 1, part_ref, below_ref, edge_sem.at[2], edge_sem.at[3], complete
    )
    send_above()
    send_below()

    for load in line:
        load.wait()
    lengths.wait()
    links.wait()
    position, live, last = line_positions(length_ref, volts_ref.shape[1])
    conductors = volts_ref.shape[0]
    set_push(volts_ref, None, work_ref, position)
    amps_load.wait()

    def keep(c, rows, total):
        amps_ref[c, rows, :] = amps_ref[c, rows, :] - total

    contract(inductance_ref, work_ref, keep)
    total = inductance_ref[0]
    for d in range(1, conductors):
        total = total + inductance_ref[d]
    sum_ref[...] = total

    rest.wait()

    def inner(layer, carry):
        magnetic_layer(field, magnetic, fresh, layer, layer + 1)
        return carry

    lax.fori_loop(0, depth - 1, inner, 0)
    cell_codes(cell_ref, halves, depth, chunks, word_ref)
    capacitance_load.wait()

    recv_ref[me] = flat_ref[pl.ds(me, 1), :]
    finish_rows()
    for row in range(count):
        drive_ref[row : row + 1, :] = recv_ref[row]

    def driven(c, carry):
        row = pl.ds(c, 1)
        new = live * (amps_ref[c] + sum_ref[row, :] * drive_ref[...])
        amps_ref[c] = new
        ends_ref[0, row, :] = jnp.sum(new * last, axis=0, keepdims=True)
        return carry

    lax.fori_loop(0, conductors, driven, 0, unroll=4)
    set_slope(amps_ref, work_ref, position)
    volts_substep(capacitance_ref, work_ref, volts_ref, volts_ref, live)
    set_push(volts_ref, drive_ref, work_ref, position)
    amps_substep(inductance_ref, work_ref, amps_ref, amps_ref, live, last, ends_ref, 1)

    cables = mesh_shape[1]
    fed_device = (
        lax.axis_index("slab"),
        (lax.axis_index("cable") + 1) % cables,
    )
    feeds = [
        pltpu.make_async_remote_copy(
            src_ref=src, dst_ref=dst, send_sem=feed_sem.at[2 * i], recv_sem=feed_sem.at[2 * i + 1],
            device_id=fed_device, device_id_type=pl.DeviceIdType.MESH,
        )
        for i, (src, dst) in enumerate([(ends_ref, fed_ref), (last_end_ref, last_fed_ref)])
    ]
    feeds[0].start()
    set_slope(amps_ref, work_ref, position)
    volts_substep(capacitance_ref, work_ref, volts_ref, volts_ref, live)
    set_push(volts_ref, drive_ref, work_ref, position)
    amps_substep(inductance_ref, work_ref, amps_ref, amps_ref, live, last, last_end_ref, 0)
    feeds[1].start()
    feeds[0].wait()
    junction(
        fed_ref, link_ref, inductance_ref, capacitance_ref, amps_ref, flat_ref,
        amps_shift_ref, volts_shift_ref,
    )
    for row in range(count):
        send_back_ref[row] = flat_ref[row : row + 1, :]
    start_back, finish_back = row_exchange(
        count, me, place, send_back_ref, recv_back_ref, send_back_sem, recv_back_sem
    )
    start_back()
    recv_back_ref[me] = flat_ref[pl.ds(me, 1), :]

    def shifted(shift_ref, d):
        row = pl.ds(d, 1)
        return jnp.where(
            position == 0, shift_ref[0, row, :],
            jnp.where(position == 1, shift_ref[1, row, :], 0.0),
        )

    def settle(d, carry):
        amps_out[d] = amps_ref[d] + shifted(amps_shift_ref, d)
        volts_ref[d] = volts_ref[d] + shifted(volts_shift_ref, d)
        return carry

    lax.fori_loop(0, conductors, settle, 0, unroll=2)
    feeds[1].wait()
    inflow_ref[...] = feed(last_fed_ref[0], link_ref[...])
    set_slope(amps_out, work_ref, position, inflow_ref)
    volts_substep(capacitance_ref, work_ref, volts_ref, volts_out, live)

    above_here()
    magnetic_layer(field, magnetic, fresh, depth - 1, depth)
    below_here()
    sigma_load.wait()
    above_sent()
    below_sent()
    finish_back()
    for row in range(count):
        induced_out[row : row + 1, :] = recv_back_ref[row]


def opening(
    mesh_shape, cells, steer, electric, magnetic, conductivity, volts, amps, inductance,
    capacitance, length, link,
):
    _, depth, ny, nz = electric.shape
    count = mesh_shape[0] * mesh_shape[1]
    conductors, segments, tubes = volts.shape
    halves = nz // LANES
    trays = cells.shape[0] // halves
    assert cells.shape[0] == count and segments == count and tubes == LANES
    hbm = pl.BlockSpec(memory_space=pl.ANY)
    lines = volts.shape
    matrix = inductance.shape
    row = (count, 1, LANES)
    edge = (2, ny, nz)
    end = (conductors, tubes)
    rows = (segments, tubes)
    scratch = [(length.shape, jnp.int32), (link.shape, jnp.int32)]
    scratch += [
        (shape, jnp.float32)
        for shape in [
            magnetic.shape, lines, lines, matrix, matrix, lines,
            rows, row, row, row, row, edge,
            rows, end, (2,) + end, (2,) + end, (1,) + end, (1,) + end,
            (2,) + end, (2,) + end, end,
        ]
    ]
    outs = [
        (cells.shape, jnp.int32), (steer.shape, jnp.float32), (rows, jnp.float32),
        ((3, depth + 1, ny, nz), jnp.float32), (magnetic.shape, jnp.float32),
        (conductivity.shape, jnp.float32), (edge, jnp.float32),
        ((halves, trays // SUBLANES, depth, ny // SUBLANES, LANES), jnp.int32),
        (lines, jnp.float32), (lines, jnp.float32),
    ]
    semaphores = [depth + 11, count, count, count, count, 4, 4]
    return pl.pallas_call(
        functools.partial(opening_kernel, mesh_shape),
        out_shape=[pltpu.VMEM(*out) for out in outs],
        in_specs=[hbm] * 11,
        out_specs=[pl.BlockSpec(memory_space=pltpu.VMEM)] * len(outs),
        scratch_shapes=[pltpu.VMEM(*kind) for kind in scratch]
        + [pltpu.SemaphoreType.DMA((number,)) for number in semaphores],
        compiler_params=pltpu.CompilerParams(
            collective_id=0, has_side_effects=True, vmem_limit_bytes=OPENING_VMEM
        ),
        name="lines_and_exchange",
    )(
        *(
            pltpu.with_memory_space_constraint(x, pltpu.HBM)
            for x in (
                cells, steer, electric, magnetic, conductivity, volts, amps, inductance,
                capacitance, length, link,
            )
        )
    )


def at_edge(rolled, axis, last):
    tile = LANES if axis == 1 else SUBLANES
    extent = rolled.shape[axis]
    if extent == tile:
        index = lax.broadcasted_iota(jnp.int32, rolled.shape, axis)
        return jnp.where(index == (tile - 1 if last else 0), 0.0, rolled)
    cut = extent - tile if last else tile
    first = lax.slice_in_dim(rolled, 0, cut, axis=axis)
    second = lax.slice_in_dim(rolled, cut, extent, axis=axis)
    edge = second if last else first
    index = lax.broadcasted_iota(jnp.int32, edge.shape, axis)
    edge = jnp.where(index == (tile - 1 if last else 0), 0.0, edge)
    return jnp.concatenate([first, edge] if last else [edge, second], axis=axis)


def ahead(x, axis):
    return at_edge(pltpu.roll(x, x.shape[axis] - 1, axis), axis, True) - x


def behind(x, axis):
    return x - at_edge(pltpu.roll(x, 1, axis), axis, False)


def contract(matrix_ref, vector_ref, finish):
    conductors, segments = vector_ref.shape[0], vector_ref.shape[1]
    tall = 32 if segments % 32 == 0 else SUBLANES
    wide = 8

    def block(i, carry):
        first = i * wide
        for start in range(0, segments, tall):
            rows = slice(start, start + tall)
            sums = [None] * wide
            for d in range(conductors):
                vector = vector_ref[d, rows, :]
                for j in range(wide):
                    term = matrix_ref[first + j, d : d + 1, :] * vector
                    sums[j] = term if d == 0 else sums[j] + term
            for j in range(wide):
                finish(first + j, rows, sums[j])
        return carry

    lax.fori_loop(0, conductors // wide, block, 0)


def line_positions(length_ref, segments):
    lanes = length_ref.shape[1]
    position = lax.broadcasted_iota(jnp.int32, (segments, lanes), 0)
    live = (position < length_ref[...]).astype(jnp.float32)
    last = (position == length_ref[...] - 1).astype(jnp.float32)
    return position, live, last


def set_push(volts_ref, drive_ref, push_ref, position):
    segments = volts_ref.shape[1]

    def one(d, carry):
        volts = volts_ref[d]
        following = jnp.where(
            position == segments - 1, 0.0, pltpu.roll(volts, segments - 1, 0)
        )
        push = following - volts
        push_ref[d] = push if drive_ref is None else push - drive_ref[...]
        return carry

    lax.fori_loop(0, volts_ref.shape[0], one, 0, unroll=4)


def set_slope(amps_ref, slope_ref, position, inflow_ref=None):
    def one(d, carry):
        amps = amps_ref[d]
        edge = 0.0 if inflow_ref is None else inflow_ref[pl.ds(d, 1), :]
        slope_ref[d] = amps - jnp.where(position == 0, edge, pltpu.roll(amps, 1, 0))
        return carry

    lax.fori_loop(0, amps_ref.shape[0], one, 0, unroll=4)


def amps_substep(inductance_ref, push_ref, old_ref, new_ref, live, last, end_ref, slot):
    ends = {}

    def finish(c, rows, total):
        new = live[rows] * (old_ref[c, rows, :] - total)
        new_ref[c, rows, :] = new
        end = jnp.sum(new * last[rows], axis=0, keepdims=True)
        if rows.start > 0:
            end = end + end_ref[slot, pl.ds(c, 1), :]
        end_ref[slot, pl.ds(c, 1), :] = end

    contract(inductance_ref, push_ref, finish)


def volts_substep(capacitance_ref, slope_ref, old_ref, new_ref, live):
    def finish(c, rows, total):
        new_ref[c, rows, :] = live[rows] * (old_ref[c, rows, :] - total)

    contract(capacitance_ref, slope_ref, finish)


def feed(end, link):
    picked = []
    for start in range(0, end.shape[0], SUBLANES):
        rows = end[start : start + SUBLANES]
        picked.append(
            jnp.take_along_axis(rows, jnp.broadcast_to(link, rows.shape), axis=1)
        )
    return jnp.concatenate(picked, axis=0)


def apply_symmetric(matrix_ref, vector):
    total = matrix_ref[0] * vector[0:1]
    for d in range(1, vector.shape[0]):
        total = total + matrix_ref[d] * vector[d : d + 1]
    return total


def junction(
    end_ref, link_ref, inductance_ref, capacitance_ref, amps_ref,
    induced_out, amps_shift_out, volts_shift_out,
):
    link = link_ref[...]
    volts0 = apply_symmetric(capacitance_ref, feed(end_ref[0], link))
    fed = apply_symmetric(capacitance_ref, feed(end_ref[1], link))
    amps0 = apply_symmetric(inductance_ref, volts0)
    spread = apply_symmetric(capacitance_ref, amps0)
    volts0 = volts0 - spread + fed
    volts1 = spread
    amps0 = amps0 + apply_symmetric(inductance_ref, volts0 - volts1)
    amps1 = apply_symmetric(inductance_ref, volts1)
    volts_shift_out[0] = volts0
    volts_shift_out[1] = volts1
    amps_shift_out[0] = amps0
    amps_shift_out[1] = amps1
    total = amps_ref[0]
    for c in range(1, amps_ref.shape[0]):
        total = total + amps_ref[c]
    position = lax.broadcasted_iota(jnp.int32, total.shape, 0)
    first = jnp.sum(amps0, axis=0, keepdims=True)
    second = jnp.sum(amps1, axis=0, keepdims=True)
    shift = jnp.where(position == 0, first, jnp.where(position == 1, second, 0.0))
    induced_out[...] = (total + shift) / amps_ref.shape[0]


def electric_kernel(
    cell_ref, tangent_ref, induced_ref, field, fresh, sigma, below_ref, word_ref,
    volts_ref, amps_ref, electric_hbm, magnetic_hbm, volts_hbm, amps_hbm,
    new_ref, merged_ref, copy_sem,
):
    _, depth, ny, nz = new_ref.shape
    halves = nz // LANES
    trays = cell_ref.shape[0] // halves
    groups = trays // SUBLANES
    copies = [
        pltpu.make_async_copy(src, dst, copy_sem.at[depth + i])
        for i, (src, dst) in enumerate(
            [(fresh, magnetic_hbm), (volts_ref, volts_hbm), (amps_ref, amps_hbm)]
        )
    ]
    for copy in copies:
        copy.start()
    for half in range(halves):
        where = pl.ds(half, trays, stride=halves)
        cells = cell_ref[where, :]
        weights = [tangent_ref[k, where, :] * induced_ref[where, :] for k in range(3)]
        sums = [jnp.zeros_like(w) for w in weights]
        for tray in range(trays):
            same = cells == cells[tray : tray + 1]
            for k in range(3):
                sums[k] = sums[k] + jnp.where(same, weights[k][tray : tray + 1], 0.0)
        for k in range(3):
            merged_ref[k, half] = sums[k]

    shift = 28 - 4 * lax.broadcasted_iota(jnp.int32, (SUBLANES, LANES), 0)

    def one_layer(layer, hy_before, hz_before):
        for chunk in range(ny // SUBLANES):
            first = chunk * SUBLANES
            rows = pl.ds(first, SUBLANES)
            hx, hy, hz = (fresh[k, layer, rows, :] for k in range(3))
            if first > 0:
                prior = pl.ds(first - 1, SUBLANES)
                dy_hz = hz - fresh[2, layer, prior, :]
                dy_hx = hx - fresh[0, layer, prior, :]
            else:
                dy_hz, dy_hx = behind(hz, 0), behind(hx, 0)
            curls = [
                dy_hz - behind(hy, 1),
                behind(hx, 1) - (hz - hz_before(rows)),
                (hy - hy_before(rows)) - dy_hx,
            ]
            conductivity = sigma[layer, rows, :]
            inverse = 1.0 / (1.0 + conductivity)
            keep = (1.0 - conductivity) * inverse
            factor = COURANT * inverse
            deposits = [[None] * halves for _ in range(3)]
            for half in range(halves):
                picks = []
                for group in range(groups):
                    word = word_ref[half, group, layer, chunk : chunk + 1, :]
                    word = jnp.left_shift(jnp.broadcast_to(word, (SUBLANES, LANES)), shift)
                    low = lax.shift_right_logical(word, 28) & (SUBLANES - 1)
                    picks.append((word < 0, low))
                for k in range(3):
                    deposit = jnp.zeros((SUBLANES, LANES), jnp.float32)
                    for group, (hit, low) in enumerate(picks):
                        part = merged_ref[k, half, group * SUBLANES : (group + 1) * SUBLANES, :]
                        deposit = jnp.where(
                            hit, jnp.take_along_axis(part, low, axis=0), deposit
                        )
                    deposits[k][half] = deposit
            for k in range(3):
                deposit = jnp.concatenate(deposits[k], axis=1)
                new_ref[k, layer, rows, :] = keep * field[k, layer, rows, :] + factor * (
                    curls[k] - deposit
                )

    def write(layer):
        return pltpu.make_async_copy(
            new_ref.at[:, layer], electric_hbm.at[:, layer], copy_sem.at[layer]
        )

    one_layer(0, lambda rows: below_ref[0, rows, :], lambda rows: below_ref[1, rows, :])
    write(0).start()

    def inner(layer, carry):
        one_layer(
            layer,
            lambda rows: fresh[1, layer - 1, rows, :],
            lambda rows: fresh[2, layer - 1, rows, :],
        )
        write(layer).start()
        return carry

    lax.fori_loop(1, depth, inner, 0)
    for layer in range(depth):
        write(layer).wait()
    for copy in copies:
        copy.wait()


def field_step(cells, tangent, induced, field, fresh, sigma, below, words, volts, amps):
    _, depth, ny, nz = fresh.shape
    halves = nz // LANES
    trays = cells.shape[0] // halves
    vmem = pl.BlockSpec(memory_space=pltpu.VMEM)
    hbm = pl.BlockSpec(memory_space=pl.ANY)
    shapes = [fresh.shape, fresh.shape, volts.shape, amps.shape]
    return pl.pallas_call(
        electric_kernel,
        out_shape=[jax.ShapeDtypeStruct(shape, jnp.float32) for shape in shapes],
        in_specs=[vmem] * 10,
        out_specs=[hbm] * len(shapes),
        scratch_shapes=[
            pltpu.VMEM(fresh.shape, jnp.float32),
            pltpu.VMEM((3, halves, trays, LANES), jnp.float32),
            pltpu.SemaphoreType.DMA((depth + 3,)),
        ],
        compiler_params=pltpu.CompilerParams(vmem_limit_bytes=CLOSING_VMEM),
        name="field_step",
    )(cells, tangent, induced, field, fresh, sigma, below, words, volts, amps)


def local(
    mesh_shape,
    electric,
    magnetic,
    conductivity,
    voltage,
    current,
    inverse_inductance,
    inverse_capacitance,
    tangent,
    sample_cell,
    tube_length,
    junction_link,
):
    cells = sample_cell.reshape(-1, LANES)
    steer = tangent.reshape(3, -1, LANES)
    handed = opening(
        mesh_shape, cells, steer, electric, magnetic, conductivity, voltage, current,
        inverse_inductance, inverse_capacitance, tube_length[None, :], junction_link[None, :],
    )
    return tuple(field_step(*handed))


def solution(mesh):
    mesh_shape = (mesh.shape["slab"], mesh.shape["cable"])
    return jax.shard_map(
        functools.partial(local, mesh_shape),
        mesh=mesh,
        in_specs=(
            P(None, AXES, None, None),
            P(None, AXES, None, None),
            P(AXES, None, None),
            P(None, None, AXES),
            P(None, None, AXES),
            P(None, None, AXES),
            P(None, None, AXES),
            P(None, AXES, None),
            P(AXES, None),
            P(AXES),
            P(AXES),
        ),
        out_specs=(
            P(None, AXES, None, None),
            P(None, AXES, None, None),
            P(None, None, AXES),
            P(None, None, AXES),
        ),
        check_vma=False,
    )
```

```python
import functools

import jax
import jax.numpy as jnp
from jax import lax
from jax.experimental import pallas as pl
from jax.experimental.pallas import tpu as pltpu
from jax.sharding import PartitionSpec as P

COURANT = 0.5
LANES = 128
SUBLANES = 8
AXES = ("slab", "cable")
OPENING_VMEM = 30 << 20
CLOSING_VMEM = 16 << 20


def everyone(mesh_shape):
    slabs, cables = mesh_shape
    count = slabs * cables
    assert count & (count - 1) == 0
    me = lax.axis_index("slab") * cables + lax.axis_index("cable")

    def partner(step):
        peer = me ^ (count - step)
        return peer, (peer // cables, peer % cables)

    return count, me, partner


def greet_all(count, partner):
    barrier = pltpu.get_barrier_semaphore()

    def greet(step, carry):
        pl.semaphore_signal(
            barrier, inc=1, device_id=partner(step)[1], device_id_type=pl.DeviceIdType.MESH,
        )
        return carry

    lax.fori_loop(1, count, greet, 0)
    return lambda: pl.semaphore_wait(barrier, count - 1)


def row_exchange(count, me, partner, send_ref, recv_ref, sems):
    def copy(src, dst, place):
        return pltpu.make_async_remote_copy(
            src_ref=src, dst_ref=dst, send_sem=sems.at[0], recv_sem=sems.at[1],
            device_id=place, device_id_type=pl.DeviceIdType.MESH,
        )

    def start(step, carry):
        peer, place = partner(step)
        copy(send_ref.at[peer], recv_ref.at[me], place).start()
        return carry

    others = pl.ds(0, count - 1)
    every = copy(send_ref.at[others], recv_ref.at[others], partner(1)[1])

    return lambda: lax.fori_loop(1, count, start, 0), every.wait_recv, every.wait_send


def edge_copy(mesh_shape, by, src, dst, send_sem, recv_sem, settle=None):
    slabs, cables = mesh_shape
    count = slabs * cables
    me = lax.axis_index("slab") * cables + lax.axis_index("cable")
    has_target = (me + by >= 0) & (me + by < count)
    has_source = (me - by >= 0) & (me - by < count)
    target = (me + by + count) % count
    copy = pltpu.make_async_remote_copy(
        src_ref=src, dst_ref=dst, send_sem=send_sem, recv_sem=recv_sem,
        device_id=(target // cables, target % cables), device_id_type=pl.DeviceIdType.MESH,
    )

    def start():
        @pl.when(has_target)
        def _():
            copy.start()

    def received():
        @pl.when(has_source)
        def _():
            copy.wait_recv()
            if settle is not None:
                settle()

        @pl.when(jnp.logical_not(has_source))
        def _():
            dst[...] = jnp.zeros(dst.shape, jnp.float32)

    def sent():
        @pl.when(has_target)
        def _():
            copy.wait_send()

    return start, received, sent


def at_edge(rolled, axis, last):
    tile = LANES if axis == 1 else SUBLANES
    extent = rolled.shape[axis]
    if extent == tile:
        index = lax.broadcasted_iota(jnp.int32, rolled.shape, axis)
        return jnp.where(index == (tile - 1 if last else 0), 0.0, rolled)
    cut = extent - tile if last else tile
    first = lax.slice_in_dim(rolled, 0, cut, axis=axis)
    second = lax.slice_in_dim(rolled, cut, extent, axis=axis)
    edge = second if last else first
    index = lax.broadcasted_iota(jnp.int32, edge.shape, axis)
    edge = jnp.where(index == (tile - 1 if last else 0), 0.0, edge)
    return jnp.concatenate([first, edge] if last else [edge, second], axis=axis)


def ahead(x, axis):
    return at_edge(pltpu.roll(x, x.shape[axis] - 1, axis), axis, True) - x


def behind(x, axis):
    return x - at_edge(pltpu.roll(x, 1, axis), axis, False)


def contract(matrix_ref, vector_ref, finish):
    conductors, segments = vector_ref.shape[0], vector_ref.shape[1]
    tall = 32 if segments % 32 == 0 else SUBLANES
    wide = 8

    def block(i, carry):
        first = i * wide
        for start in range(0, segments, tall):
            rows = slice(start, start + tall)
            sums = [None] * wide
            for d in range(conductors):
                vector = vector_ref[d, rows, :]
                for j in range(wide):
                    term = matrix_ref[first + j, d : d + 1, :] * vector
                    sums[j] = term if d == 0 else sums[j] + term
            for j in range(wide):
                finish(first + j, rows, sums[j])
        return carry

    lax.fori_loop(0, conductors // wide, block, 0)


def line_positions(length_ref, segments):
    lanes = length_ref.shape[1]
    position = lax.broadcasted_iota(jnp.int32, (segments, lanes), 0)
    live = (position < length_ref[...]).astype(jnp.float32)
    last = (position == length_ref[...] - 1).astype(jnp.float32)
    return position, live, last


def set_push(volts_ref, drive_ref, push_ref, position):
    segments = volts_ref.shape[1]

    def one(d, carry):
        volts = volts_ref[d]
        following = jnp.where(
            position == segments - 1, 0.0, pltpu.roll(volts, segments - 1, 0)
        )
        push = following - volts
        push_ref[d] = push if drive_ref is None else push - drive_ref[...]
        return carry

    lax.fori_loop(0, volts_ref.shape[0], one, 0, unroll=4)


def set_slope(amps_ref, slope_ref, position, inflow_ref=None):
    def one(d, carry):
        amps = amps_ref[d]
        edge = 0.0 if inflow_ref is None else inflow_ref[pl.ds(d, 1), :]
        slope_ref[d] = amps - jnp.where(position == 0, edge, pltpu.roll(amps, 1, 0))
        return carry

    lax.fori_loop(0, amps_ref.shape[0], one, 0, unroll=4)


def amps_substep(inductance_ref, push_ref, old_ref, new_ref, live, last, end_ref):
    def finish(c, rows, total):
        new = live[rows] * (old_ref[c, rows, :] - total)
        new_ref[c, rows, :] = new
        if end_ref is None:
            return
        end = jnp.sum(new * last[rows], axis=0, keepdims=True)
        if rows.start > 0:
            end = end + end_ref[pl.ds(c, 1), :]
        end_ref[pl.ds(c, 1), :] = end

    contract(inductance_ref, push_ref, finish)


def volts_substep(capacitance_ref, slope_ref, old_ref, new_ref, live):
    def finish(c, rows, total):
        new_ref[c, rows, :] = live[rows] * (old_ref[c, rows, :] - total)

    contract(capacitance_ref, slope_ref, finish)


def feed(end, link):
    picked = []
    for start in range(0, end.shape[0], SUBLANES):
        rows = end[start : start + SUBLANES]
        picked.append(
            jnp.take_along_axis(rows, jnp.broadcast_to(link, rows.shape), axis=1)
        )
    return jnp.concatenate(picked, axis=0)


def apply_symmetric(matrix_ref, vector):
    total = matrix_ref[0] * vector[0:1]
    for d in range(1, vector.shape[0]):
        total = total + matrix_ref[d] * vector[d : d + 1]
    return total


def junction(
    first, second, inductance_ref, capacitance_ref, amps_shift_ref, volts_shift_ref,
):
    volts0 = apply_symmetric(capacitance_ref, first)
    fed = apply_symmetric(capacitance_ref, second)
    amps0 = apply_symmetric(inductance_ref, volts0)
    spread = apply_symmetric(capacitance_ref, amps0)
    volts0 = volts0 - spread + fed
    volts1 = spread
    amps0 = amps0 + apply_symmetric(inductance_ref, volts0 - volts1)
    amps1 = apply_symmetric(inductance_ref, volts1)
    volts_shift_ref[0] = volts0
    volts_shift_ref[1] = volts1
    amps_shift_ref[0] = amps0
    amps_shift_ref[1] = amps1


def segment_steps(position, live):
    segments = position.shape[0]

    def back(x):
        return x - jnp.where(position == 0, 0.0, pltpu.roll(x, 1, 0))

    def forth(x):
        return jnp.where(position == segments - 1, 0.0, pltpu.roll(x, segments - 1, 0)) - x

    return back, forth


def current_sums(dots, sums, drive, position, live, starts):
    back, forth = segment_steps(position, live)
    amps, volts = list(dots[:3]), list(dots[3:])
    starts = [jnp.where(position == 0, x, 0.0) for x in starts]
    pull = [s * drive for s in sums]
    amps = [live * (a - forth(v) + p) for a, v, p in zip(amps, volts, pull)]
    volts = [live * (volts[i] - back(amps[i + 1]) + starts[i]) for i in range(2)]
    amps = [live * (amps[i] - forth(volts[i]) + pull[i]) for i in range(2)]
    volts = live * (volts[0] - back(amps[1]) + starts[2])
    return live * (amps[0] - forth(volts) + pull[0])


def responses(drive, position, live):
    back, forth = segment_steps(position, live)
    p1 = live * drive
    q1 = live * back(p1)
    p2 = live * forth(q1)
    q2 = live * back(p2)
    p3 = live * forth(q2)
    return p1, p2, p3, q1, q2


def partial_edge(field, magnetic, layer, part):
    ny = field.shape[2]
    for first in range(0, ny, SUBLANES):
        rows = pl.ds(first, SUBLANES)
        ex, ey, ez = (field[k, layer, rows, :] for k in range(3))
        if first + SUBLANES < ny:
            dy_ex = field[0, layer, pl.ds(first + 1, SUBLANES), :] - ex
        else:
            dy_ex = ahead(ex, 0)
        part[0, rows, :] = magnetic[1, layer, rows, :] - COURANT * (ahead(ex, 1) + ez)
        part[1, rows, :] = magnetic[2, layer, rows, :] + COURANT * (ey + dy_ex)


def magnetic_layer(field, magnetic, fresh, layer, following):
    ny = field.shape[2]
    for first in range(0, ny, SUBLANES):
        rows = pl.ds(first, SUBLANES)
        ex, ey, ez = (field[k, layer, rows, :] for k in range(3))
        if first + SUBLANES < ny:
            after = pl.ds(first + 1, SUBLANES)
            dy_ez = field[2, layer, after, :] - ez
            dy_ex = field[0, layer, after, :] - ex
        else:
            dy_ez, dy_ex = ahead(ez, 0), ahead(ex, 0)
        dx_ez = field[2, following, rows, :] - ez
        dx_ey = field[1, following, rows, :] - ey
        fresh[0, layer, rows, :] = magnetic[0, layer, rows, :] - COURANT * (dy_ez - ahead(ey, 1))
        fresh[1, layer, rows, :] = magnetic[1, layer, rows, :] - COURANT * (ahead(ex, 1) - dx_ez)
        fresh[2, layer, rows, :] = magnetic[2, layer, rows, :] - COURANT * (dx_ey - dy_ex)


def opening_kernel(
    mesh_shape, cell_hbm, tangent_hbm, electric_hbm, magnetic_hbm, conductivity_hbm,
    volts_hbm, amps_hbm, inductance_hbm, capacitance_hbm, length_hbm, link_hbm,
    cell_ref, tangent_ref, induced_out, field, sigma, fresh, below_ref, volts_out, amps_out,
    inflow_ref, capacitance_ref, length_ref,
    link_ref, magnetic, volts_ref, amps_ref, inductance_ref,
    work_ref, flat_ref, send_ref, recv_ref, send_back_ref, recv_back_ref, part_ref,
    drive_ref, fixed_ref, even_ref, sent_ref, fixed_fed_ref, ends_ref, dot_ref, last_end_ref,
    last_fed_ref, amps_shift_ref, volts_shift_ref, response_ref,
    load_sem, row_sem, back_sem, edge_sem, feed_sem,
):
    depth, ny, nz = magnetic.shape[1:]
    count, me, partner = everyone(mesh_shape)
    cables = mesh_shape[1]

    def load(i, src, dst):
        copy = pltpu.make_async_copy(src, dst, load_sem.at[i])
        copy.start()
        return copy.wait

    cells_loaded, tangent_loaded = load(0, cell_hbm, cell_ref), load(1, tangent_hbm, tangent_ref)
    base = 2 + depth

    def layer_copy(i):
        return pltpu.make_async_copy(electric_hbm.at[:, i], field.at[:, i], load_sem.at[2 + i])

    for i in range(depth):
        layer_copy(i).start()
    lines = [
        load(base + i, src, dst)
        for i, (src, dst) in enumerate([
            (length_hbm, length_ref), (link_hbm, link_ref), (inductance_hbm, inductance_ref),
            (capacitance_hbm, capacitance_ref), (volts_hbm, volts_ref), (amps_hbm, amps_ref),
        ])
    ]
    last_layer = depth - 1
    magnetic_top = load(
        base + 6, magnetic_hbm.at[:, last_layer], magnetic.at[:, last_layer]
    )
    greeted = greet_all(count, partner)
    conductors, segments = volts_ref.shape[:2]
    halves = nz // LANES
    trays = cell_ref.shape[0] // halves
    groups = trays // SUBLANES
    chunks = ny // SUBLANES
    cells_loaded()

    def sample(layer, found):
        layer_copy(layer).wait()
        found = list(found)
        for half in range(halves):
            spots = []
            for group in range(groups):
                start = group * SUBLANES * halves + half
                cells = cell_ref[pl.ds(start, SUBLANES, stride=halves), :]
                spots.append((cells & (SUBLANES - 1), (cells >> 3) - layer * chunks))
            for chunk in range(chunks):
                rows = slice(chunk * SUBLANES, (chunk + 1) * SUBLANES)
                tiles = [
                    field[k, layer, rows, half * LANES : (half + 1) * LANES] for k in range(3)
                ]
                for group, (low, high) in enumerate(spots):
                    hit = high == chunk
                    for k in range(3):
                        at = (half * groups + group) * 3 + k
                        value = jnp.take_along_axis(tiles[k], low, axis=0)
                        found[at] = jnp.where(hit, value, found[at])
        return tuple(found)

    nothing = (jnp.zeros((SUBLANES, LANES), jnp.float32),) * (3 * halves * groups)
    found = lax.fori_loop(0, depth, sample, nothing)
    tangent_loaded()
    for half in range(halves):
        for group in range(groups):
            where = pl.ds(group * SUBLANES * halves + half, SUBLANES, stride=halves)
            at = (half * groups + group) * 3
            x, y, z = found[at : at + 3]
            flat_ref[where, :] = (
                tangent_ref[0, where, :] * x
                + tangent_ref[1, where, :] * y
                + tangent_ref[2, where, :] * z
            )
    for row in range(count):
        source = row // cables * cables + (row % cables + cables - 1) % cables
        send_ref[row, 0:1] = flat_ref[row : row + 1, :]
        send_ref[row, 1:2] = flat_ref[source : source + 1, :]
    start_rows, rows_here, rows_sent = row_exchange(
        count, me, partner, send_ref, recv_ref, row_sem
    )
    rest = pl.ds(0, last_layer)
    magnetic_rest = load(base + 7, magnetic_hbm.at[:, rest], magnetic.at[:, rest])
    sigma_loaded = load(base + 8, conductivity_hbm, sigma)
    for wait in lines:
        wait()
    position, live, last = line_positions(length_ref, segments)
    beyond = (position == length_ref[...]).astype(jnp.float32)
    before_last = (position == length_ref[...] - 2).astype(jnp.float32)
    spread = inductance_ref[0]
    for d in range(1, conductors):
        spread = spread + inductance_ref[d]
    fixed_ref[0] = spread
    for i in range(2):
        even_ref[i] = apply_symmetric(capacitance_ref, fixed_ref[i])
        fixed_ref[i + 1] = apply_symmetric(inductance_ref, even_ref[i])
    sent_ref[0, 0:1] = length_ref[...].astype(jnp.float32)
    sent_ref[1] = fixed_ref[0]
    sent_ref[2] = fixed_ref[1]
    last_end_ref[1] = fixed_ref[2]

    def gather_ends(c, carry):
        row = pl.ds(c, 1)
        volts, amps = volts_ref[c], amps_ref[c]
        picks = (
            volts * beyond, volts * last, volts * before_last, amps * last, amps * before_last
        )
        for i, x in enumerate(picks):
            ends_ref[i, row, :] = jnp.sum(x, axis=0, keepdims=True)
        terms = [amps]
        terms += [even_ref[i, row, :] * amps for i in range(2)]
        terms += [fixed_ref[i, row, :] * volts for i in range(3)]
        return tuple(x + y for x, y in zip(carry, terms))

    zero = jnp.zeros((segments, LANES), jnp.float32)
    dots = lax.fori_loop(0, conductors, gather_ends, (zero,) * 6, unroll=2)
    for i, x in enumerate(dots):
        dot_ref[i] = x
    at_last, at_before = ends_ref[1], ends_ref[2]
    amps_last = ends_ref[3] - apply_symmetric(inductance_ref, ends_ref[0] - at_last)
    amps_before = ends_ref[4] - apply_symmetric(inductance_ref, at_last - at_before)
    volts_last = at_last - apply_symmetric(capacitance_ref, amps_last - amps_before)
    sent_ref[3] = amps_last
    sent_ref[4] = amps_last + apply_symmetric(inductance_ref, volts_last)

    fed_device = (lax.axis_index("slab"), (lax.axis_index("cable") + 1) % cables)
    fixed_feed, last_feed = [
        pltpu.make_async_remote_copy(
            src_ref=src, dst_ref=dst, send_sem=feed_sem.at[2 * i], recv_sem=feed_sem.at[2 * i + 1],
            device_id=fed_device, device_id_type=pl.DeviceIdType.MESH,
        )
        for i, (src, dst) in enumerate(
            [(sent_ref, fixed_fed_ref), (last_end_ref, last_fed_ref)]
        )
    ]
    greeted()
    start_rows()
    recv_ref[me] = send_ref[me]

    fixed_feed.start()
    magnetic_top()
    partial_edge(field, magnetic, last_layer, part_ref)

    def complete():
        for first in range(0, ny, SUBLANES):
            rows = pl.ds(first, SUBLANES)
            below_ref[0, rows, :] = below_ref[0, rows, :] + COURANT * field[2, 0, rows, :]
            below_ref[1, rows, :] = below_ref[1, rows, :] - COURANT * field[1, 0, rows, :]

    send_above, above_here, above_sent = edge_copy(
        mesh_shape, -1, field.at[pl.ds(1, 2), 0], field.at[pl.ds(1, 2), depth],
        edge_sem.at[0], edge_sem.at[1],
    )
    send_below, below_here, below_sent = edge_copy(
        mesh_shape, 1, part_ref, below_ref, edge_sem.at[2], edge_sem.at[3], complete
    )
    send_above()
    send_below()


    def amps_step(ends=None):
        set_push(volts_ref, None, work_ref, position)
        amps_substep(inductance_ref, work_ref, amps_ref, amps_ref, live, last, ends)

    def volts_step():
        set_slope(amps_ref, work_ref, position)
        volts_substep(capacitance_ref, work_ref, volts_ref, volts_ref, live)

    amps_step()
    volts_step()
    amps_step()
    link = link_ref[...]
    sums = [jnp.sum(fixed_ref[i], axis=0, keepdims=True) for i in range(3)]
    fixed_feed.wait()
    fed1, fed3, first, second = (feed(fixed_fed_ref[i], link) for i in range(1, 5))
    fed_length = fixed_fed_ref[0, 0:1].astype(jnp.int32)
    fed_live = (position < fed_length).astype(jnp.float32)
    fed_last = (position == fed_length - 1).astype(jnp.float32)

    rows_here()
    for row in range(count):
        drive_ref[0, row : row + 1, :] = recv_ref[row, 0:1]
        drive_ref[1, row : row + 1, :] = recv_ref[row, 1:2]
    e1, e2, e3 = (
        feed(jnp.broadcast_to(jnp.sum(p * fed_last, axis=0, keepdims=True), link_rows), link)
        for link_rows in [(SUBLANES, LANES)]
        for p in responses(drive_ref[1], position, fed_live)[:3]
    )
    e1, e2, e3 = e1[0:1], e2[0:1], e3[0:1]
    first = first + fed1 * e1
    second = second + 2.0 * fed1 * e1 + fed3 * e2
    flat_ref[...] = current_sums(
        [dot_ref[i] for i in range(6)], sums, drive_ref[0], position, live,
        [jnp.sum(x * y, axis=0, keepdims=True)
         for x, y in ((even_ref[0], first), (even_ref[1], first), (even_ref[0], second))],
    ) / conductors
    for row in range(count):
        send_back_ref[row] = flat_ref[row : row + 1, :]
    start_back, back_here, back_sent = row_exchange(
        count, me, partner, send_back_ref, recv_back_ref, back_sem
    )
    start_back()
    recv_back_ref[me] = flat_ref[pl.ds(me, 1), :]

    p1, p2, p3, q1, q2 = responses(drive_ref[0], position, live)
    for i, x in enumerate((3.0 * p1, 4.0 * p2, p3, 3.0 * q1, q2)):
        response_ref[i] = x
    volts_step()
    amps_step(last_end_ref.at[0])
    last_feed.start()
    junction(first, second, inductance_ref, capacitance_ref, amps_shift_ref, volts_shift_ref)
    magnetic_rest()

    def inner(layer, carry):
        magnetic_layer(field, magnetic, fresh, layer, layer + 1)
        return carry

    lax.fori_loop(0, last_layer, inner, 0)
    last_feed.wait()
    inflow_ref[...] = (
        feed(last_fed_ref[0], link) + 3.0 * fed1 * e1 + 4.0 * fed3 * e2
        + feed(last_fed_ref[1], link) * e3
    )

    def shifted(shift_ref, row):
        return jnp.where(
            position == 0, shift_ref[0, row, :],
            jnp.where(position == 1, shift_ref[1, row, :], 0.0),
        )

    def settle(d, carry):
        row = pl.ds(d, 1)
        amps = amps_ref[d] + shifted(amps_shift_ref, row)
        for i in range(3):
            amps = amps + fixed_ref[i, row, :] * response_ref[i]
        amps_out[d] = amps
        volts = volts_ref[d] + shifted(volts_shift_ref, row)
        for i in range(2):
            volts = volts - even_ref[i, row, :] * response_ref[3 + i]
        volts_out[d] = volts
        return carry

    lax.fori_loop(0, conductors, settle, 0, unroll=2)
    above_here()
    magnetic_layer(field, magnetic, fresh, last_layer, depth)
    below_here()
    sigma_loaded()
    above_sent()
    below_sent()
    rows_sent()
    back_sent()
    back_here()
    for row in range(count):
        induced_out[row : row + 1, :] = recv_back_ref[row]


def opening(
    mesh_shape, cells, steer, electric, magnetic, conductivity, volts, amps, inductance,
    capacitance, length, link,
):
    _, depth, ny, nz = electric.shape
    count = mesh_shape[0] * mesh_shape[1]
    conductors, segments, tubes = volts.shape
    assert cells.shape[0] == count and segments == count and tubes == LANES
    hbm = pl.BlockSpec(memory_space=pl.ANY)
    lines = volts.shape
    matrix = inductance.shape
    edge = (2, ny, nz)
    end = (conductors, tubes)
    rows = (segments, tubes)
    scratch = [(link.shape, jnp.int32)]
    scratch += [
        (shape, jnp.float32)
        for shape in [
            magnetic.shape, lines, lines, matrix,
            lines, rows, (count, 2, LANES), (count, 2, LANES), (count, 1, LANES),
            (count, 1, LANES), edge,
            (2,) + rows, (3,) + end, (2,) + end, (5,) + end, (5,) + end, (5,) + end, (6,) + rows,
            (2,) + end, (2,) + end, (2,) + end, (2,) + end, (5,) + rows,
        ]
    ]
    outs = [
        (cells.shape, jnp.int32), (steer.shape, jnp.float32), (rows, jnp.float32),
        ((3, depth + 1, ny, nz), jnp.float32), (conductivity.shape, jnp.float32),
        (magnetic.shape, jnp.float32), (edge, jnp.float32), (lines, jnp.float32),
        (lines, jnp.float32), (end, jnp.float32), (matrix, jnp.float32),
        (length.shape, jnp.int32),
    ]
    semaphores = [depth + 11, 2, 2, 4, 4]
    return pl.pallas_call(
        functools.partial(opening_kernel, mesh_shape),
        out_shape=[pltpu.VMEM(*out) for out in outs],
        in_specs=[hbm] * 11,
        out_specs=[pl.BlockSpec(memory_space=pltpu.VMEM)] * len(outs),
        scratch_shapes=[pltpu.VMEM(*kind) for kind in scratch]
        + [pltpu.SemaphoreType.DMA((number,)) for number in semaphores],
        compiler_params=pltpu.CompilerParams(
            collective_id=0, has_side_effects=True, vmem_limit_bytes=OPENING_VMEM
        ),
        name="lines_and_exchange",
    )(
        *(
            pltpu.with_memory_space_constraint(x, pltpu.HBM)
            for x in (
                cells, steer, electric, magnetic, conductivity, volts, amps, inductance,
                capacitance, length, link,
            )
        )
    )


def electric_kernel(
    cell_ref, tangent_ref, induced_ref, field, sigma, fresh, below_ref, volts_ref, amps_ref,
    inflow_ref, capacitance_ref, length_ref,
    electric_hbm, magnetic_hbm, volts_hbm, amps_hbm,
    new_ref, volts_new, work_ref, word_ref, merged_ref, copy_sem,
):
    _, depth, ny, nz = new_ref.shape
    halves = nz // LANES
    trays = cell_ref.shape[0] // halves
    groups = trays // SUBLANES
    chunks = ny // SUBLANES
    copies = [
        pltpu.make_async_copy(src, dst, copy_sem.at[depth + i])
        for i, (src, dst) in enumerate(
            [(fresh, magnetic_hbm), (amps_ref, amps_hbm), (volts_new, volts_hbm)]
        )
    ]
    for copy in copies[:2]:
        copy.start()
    position, live, _ = line_positions(length_ref, volts_ref.shape[1])
    set_slope(amps_ref, work_ref, position, inflow_ref)
    volts_substep(capacitance_ref, work_ref, volts_ref, volts_new, live)
    copies[2].start()
    kept = []
    for half in range(halves):
        where = pl.ds(half, trays, stride=halves)
        cells = cell_ref[where, :]
        weights = [tangent_ref[k, where, :] * induced_ref[where, :] for k in range(3)]
        sums = [jnp.zeros_like(w) for w in weights]
        order = lax.broadcasted_iota(jnp.int32, cells.shape, 0)
        late = jnp.zeros(cells.shape, jnp.int32)
        for tray in range(trays):
            same = cells == cells[tray : tray + 1]
            late = jnp.where(same & (order > tray), 1, late)
            for k in range(3):
                sums[k] = sums[k] + jnp.where(same, weights[k][tray : tray + 1], 0.0)
        for k in range(3):
            merged_ref[k, half] = sums[k]
        block = jnp.where(late == 0, cells >> 3, -1)
        code = jnp.left_shift((order & (SUBLANES - 1)) | SUBLANES, (cells & (SUBLANES - 1)) * 4)
        kept.append((block, code))

    shift = 28 - 4 * lax.broadcasted_iota(jnp.int32, (SUBLANES, LANES), 0)

    def write(layer):
        return pltpu.make_async_copy(
            new_ref.at[:, layer], electric_hbm.at[:, layer], copy_sem.at[layer]
        )

    def one_layer(layer, hy_before, hz_before):
        here = lax.broadcasted_iota(jnp.int32, (chunks, LANES), 0) + layer * chunks
        for half in range(halves):
            block, code = kept[half]
            for group in range(groups):
                word = jnp.zeros((chunks, LANES), jnp.int32)
                for tray in range(group * SUBLANES, (group + 1) * SUBLANES):
                    hit = block[tray : tray + 1] == here
                    word = word | jnp.where(hit, code[tray : tray + 1], 0)
                word_ref[half, group] = word
        for chunk in range(chunks):
            first = chunk * SUBLANES
            rows = pl.ds(first, SUBLANES)
            hx, hy, hz = (fresh[k, layer, rows, :] for k in range(3))
            if first > 0:
                prior = pl.ds(first - 1, SUBLANES)
                dy_hz = hz - fresh[2, layer, prior, :]
                dy_hx = hx - fresh[0, layer, prior, :]
            else:
                dy_hz, dy_hx = behind(hz, 0), behind(hx, 0)
            curls = [
                dy_hz - behind(hy, 1),
                behind(hx, 1) - (hz - hz_before(rows)),
                (hy - hy_before(rows)) - dy_hx,
            ]
            conductivity = sigma[layer, rows, :]
            inverse = 1.0 / (1.0 + conductivity)
            keep = (1.0 - conductivity) * inverse
            factor = COURANT * inverse
            deposits = [[None] * halves for _ in range(3)]
            for half in range(halves):
                picks = []
                for group in range(groups):
                    word = word_ref[half, group, chunk : chunk + 1, :]
                    word = jnp.left_shift(jnp.broadcast_to(word, (SUBLANES, LANES)), shift)
                    low = lax.shift_right_logical(word, 28) & (SUBLANES - 1)
                    picks.append((word < 0, low))
                for k in range(3):
                    deposit = jnp.zeros((SUBLANES, LANES), jnp.float32)
                    for group, (hit, low) in enumerate(picks):
                        part = merged_ref[k, half, group * SUBLANES : (group + 1) * SUBLANES, :]
                        deposit = jnp.where(
                            hit, jnp.take_along_axis(part, low, axis=0), deposit
                        )
                    deposits[k][half] = deposit
            for k in range(3):
                deposit = jnp.concatenate(deposits[k], axis=1)
                new_ref[k, layer, rows, :] = keep * field[k, layer, rows, :] + factor * (
                    curls[k] - deposit
                )
        write(layer).start()

    one_layer(0, lambda rows: below_ref[0, rows, :], lambda rows: below_ref[1, rows, :])

    def inner(layer, carry):
        one_layer(
            layer,
            lambda rows: fresh[1, layer - 1, rows, :],
            lambda rows: fresh[2, layer - 1, rows, :],
        )
        return carry

    lax.fori_loop(1, depth, inner, 0)
    for layer in range(depth):
        write(layer).wait()
    for copy in copies:
        copy.wait()


def field_step(*handed):
    cells, fresh, volts, amps = handed[0], handed[5], handed[7], handed[8]
    _, depth, ny, nz = fresh.shape
    halves = nz // LANES
    trays = cells.shape[0] // halves
    vmem = pl.BlockSpec(memory_space=pltpu.VMEM)
    hbm = pl.BlockSpec(memory_space=pl.ANY)
    shapes = [fresh.shape, fresh.shape, volts.shape, amps.shape]
    return pl.pallas_call(
        electric_kernel,
        out_shape=[jax.ShapeDtypeStruct(shape, jnp.float32) for shape in shapes],
        in_specs=[vmem] * len(handed),
        out_specs=[hbm] * len(shapes),
        scratch_shapes=[
            pltpu.VMEM(fresh.shape, jnp.float32),
            pltpu.VMEM(volts.shape, jnp.float32),
            pltpu.VMEM(volts.shape, jnp.float32),
            pltpu.VMEM((halves, trays // SUBLANES, ny // SUBLANES, LANES), jnp.int32),
            pltpu.VMEM((3, halves, trays, LANES), jnp.float32),
            pltpu.SemaphoreType.DMA((depth + 3,)),
        ],
        compiler_params=pltpu.CompilerParams(vmem_limit_bytes=CLOSING_VMEM),
        name="field_step",
    )(*handed)


def local(
    mesh_shape,
    electric,
    magnetic,
    conductivity,
    voltage,
    current,
    inverse_inductance,
    inverse_capacitance,
    tangent,
    sample_cell,
    tube_length,
    junction_link,
):
    cells = sample_cell.reshape(-1, LANES)
    steer = tangent.reshape(3, -1, LANES)
    handed = opening(
        mesh_shape, cells, steer, electric, magnetic, conductivity, voltage, current,
        inverse_inductance, inverse_capacitance, tube_length[None, :], junction_link[None, :],
    )
    return tuple(field_step(*handed))


def solution(mesh):
    mesh_shape = (mesh.shape["slab"], mesh.shape["cable"])
    return jax.shard_map(
        functools.partial(local, mesh_shape),
        mesh=mesh,
        in_specs=(
            P(None, AXES, None, None),
            P(None, AXES, None, None),
            P(AXES, None, None),
            P(None, None, AXES),
            P(None, None, AXES),
            P(None, None, AXES),
            P(None, None, AXES),
            P(None, AXES, None),
            P(AXES, None),
            P(AXES),
            P(AXES),
        ),
        out_specs=(
            P(None, AXES, None, None),
            P(None, AXES, None, None),
            P(None, None, AXES),
            P(None, None, AXES),
        ),
        check_vma=False,
    )
```

```python
import functools

import jax
import jax.numpy as jnp
from jax import lax
from jax.experimental import pallas as pl
from jax.experimental.pallas import tpu as pltpu
from jax.sharding import PartitionSpec as P

COURANT = 0.5
LANES = 128
SUBLANES = 8
AXES = ("slab", "cable")
OPENING_VMEM = 30 << 20
CLOSING_VMEM = 8 << 20
WIDE = 32
BANDS = 4
EARLY_BANDS = 1


def everyone(mesh_shape):
    slabs, cables = mesh_shape
    count = slabs * cables
    assert count & (count - 1) == 0
    me = lax.axis_index("slab") * cables + lax.axis_index("cable")

    def partner(step):
        peer = me ^ (count - step)
        return peer, (peer // cables, peer % cables)

    return count, me, partner


def greet_all(count, partner):
    barrier = pltpu.get_barrier_semaphore()

    def greet(step, carry):
        pl.semaphore_signal(
            barrier, inc=1, device_id=partner(step)[1], device_id_type=pl.DeviceIdType.MESH,
        )
        return carry

    lax.fori_loop(1, count, greet, 0)
    return lambda: pl.semaphore_wait(barrier, count - 1)


def row_exchange(count, me, partner, send_ref, recv_ref, sems):
    def copy(src, dst, place):
        return pltpu.make_async_remote_copy(
            src_ref=src, dst_ref=dst, send_sem=sems.at[0], recv_sem=sems.at[1],
            device_id=place, device_id_type=pl.DeviceIdType.MESH,
        )

    def start(step, carry):
        peer, place = partner(step)
        copy(send_ref.at[peer], recv_ref.at[me], place).start()
        return carry

    others = pl.ds(0, count - 1)
    every = copy(send_ref.at[others], recv_ref.at[others], partner(1)[1])

    return lambda: lax.fori_loop(1, count, start, 0), every.wait_recv, every.wait_send


def edge_copy(mesh_shape, by, src, dst, send_sem, recv_sem, settle=None):
    slabs, cables = mesh_shape
    count = slabs * cables
    me = lax.axis_index("slab") * cables + lax.axis_index("cable")
    has_target = (me + by >= 0) & (me + by < count)
    has_source = (me - by >= 0) & (me - by < count)
    target = (me + by + count) % count
    copy = pltpu.make_async_remote_copy(
        src_ref=src, dst_ref=dst, send_sem=send_sem, recv_sem=recv_sem,
        device_id=(target // cables, target % cables), device_id_type=pl.DeviceIdType.MESH,
    )

    def start():
        @pl.when(has_target)
        def _():
            copy.start()

    def received():
        @pl.when(has_source)
        def _():
            copy.wait_recv()
            if settle is not None:
                settle()

        @pl.when(jnp.logical_not(has_source))
        def _():
            dst[...] = jnp.zeros(dst.shape, jnp.float32)

    def sent():
        @pl.when(has_target)
        def _():
            copy.wait_send()

    return start, received, sent


def at_edge(rolled, axis, last):
    tile = LANES if axis == 1 else SUBLANES
    extent = rolled.shape[axis]
    if extent == tile:
        index = lax.broadcasted_iota(jnp.int32, rolled.shape, axis)
        return jnp.where(index == (tile - 1 if last else 0), 0.0, rolled)
    cut = extent - tile if last else tile
    first = lax.slice_in_dim(rolled, 0, cut, axis=axis)
    second = lax.slice_in_dim(rolled, cut, extent, axis=axis)
    edge = second if last else first
    index = lax.broadcasted_iota(jnp.int32, edge.shape, axis)
    edge = jnp.where(index == (tile - 1 if last else 0), 0.0, edge)
    return jnp.concatenate([first, edge] if last else [edge, second], axis=axis)


def ahead(x, axis):
    return at_edge(pltpu.roll(x, x.shape[axis] - 1, axis), axis, True) - x


def behind(x, axis):
    return x - at_edge(pltpu.roll(x, 1, axis), axis, False)


def line_positions(length_ref, segments):
    lanes = length_ref.shape[1]
    position = lax.broadcasted_iota(jnp.int32, (segments, lanes), 0)
    live = (position < length_ref[...]).astype(jnp.float32)
    last = (position == length_ref[...] - 1).astype(jnp.float32)
    return position, live, last


def feed(end, link):
    picked = []
    for start in range(0, end.shape[0], SUBLANES):
        rows = end[start : start + SUBLANES]
        picked.append(
            jnp.take_along_axis(rows, jnp.broadcast_to(link, rows.shape), axis=1)
        )
    return jnp.concatenate(picked, axis=0)


def apply_symmetric(matrix_ref, vector):
    total = matrix_ref[0] * vector[0:1]
    for d in range(1, vector.shape[0]):
        total = total + matrix_ref[d] * vector[d : d + 1]
    return total


def junction(
    first, second, third, inductance_ref, capacitance_ref, amps_shift_ref, volts_shift_ref,
):
    volts0 = apply_symmetric(capacitance_ref, first)
    fed = apply_symmetric(capacitance_ref, second)
    amps0 = apply_symmetric(inductance_ref, volts0)
    spread = apply_symmetric(capacitance_ref, amps0)
    volts0 = volts0 - spread + fed
    volts1 = spread
    amps0 = amps0 + apply_symmetric(inductance_ref, volts0 - volts1)
    amps1 = apply_symmetric(inductance_ref, volts1)
    amps_shift_ref[0] = amps0
    amps_shift_ref[1] = amps1
    volts_shift_ref[0] = volts0 - apply_symmetric(capacitance_ref, amps0 - third)
    volts_shift_ref[1] = volts1 - apply_symmetric(capacitance_ref, amps1 - amps0)
    volts_shift_ref[2] = apply_symmetric(capacitance_ref, amps1)


def turn_pieces(tiles):
    number = len(tiles)
    piece = lax.broadcasted_iota(jnp.int32, (SUBLANES, LANES), 1) // (LANES // number)
    bit = 1
    while bit < number:
        odd = (piece & bit) != 0
        tiles = [jnp.where(odd, tiles[(i + bit) % number], tiles[i]) for i in range(number)]
        bit *= 2
    return [tiles[-i % number] for i in range(number)]


def by_group(src_ref, dst_ref):
    number, rows = src_ref.shape[:2]
    width = LANES // number

    def one(r, carry):
        here = pl.ds(pl.multiple_of(r * SUBLANES, SUBLANES), SUBLANES)
        tiles = [src_ref[0, here, :]]
        for i in range(1, number):
            tiles.append(pltpu.roll(src_ref[i, here, :], width * i, 1))
        for i, tile in enumerate(turn_pieces(tiles)):
            dst_ref[i, here, :] = tile
        return carry

    lax.fori_loop(0, rows // SUBLANES, one, 0, unroll=4)


def by_conductor(src_ref, dst_ref):
    number, rows = src_ref.shape[:2]
    width = LANES // number

    def one(r, carry):
        here = pl.ds(pl.multiple_of(r * SUBLANES, SUBLANES), SUBLANES)
        tiles = turn_pieces([src_ref[i, here, :] for i in range(number)])
        dst_ref[0, here, :] = tiles[0]
        for i in range(1, number):
            dst_ref[i, here, :] = pltpu.roll(tiles[i], LANES - width * i, 1)
        return carry

    lax.fori_loop(0, rows // SUBLANES, one, 0, unroll=4)


def spread_weights(src_ref, twice_ref, weight_ref):
    groups, conductors = src_ref.shape[:2]
    width = LANES // conductors
    lane = lax.broadcasted_iota(jnp.int32, (SUBLANES, LANES), 1)
    sub = lax.broadcasted_iota(jnp.int32, (SUBLANES, LANES), 0)
    diagonal = (lane % width) == (sub % width)
    source = [(j * SUBLANES + sub) // width for j in range(width)]

    def one(g, carry):
        slot = lax.rem(g, twice_ref.shape[0])
        for base in range(0, 2 * conductors, conductors):
            twice_ref[slot, base : base + conductors, :] = src_ref[g]
        for r in range(0, conductors, SUBLANES):
            x = twice_ref[slot, pl.ds(conductors - g + r, SUBLANES), :]
            high = x.astype(jnp.bfloat16).astype(jnp.float32)
            for base, part in ((0, high), (LANES, x - high)):
                rows = [
                    jnp.where(diagonal, jnp.take_along_axis(part, s, axis=0), 0.0) for s in source
                ]
                block = jnp.concatenate(rows, axis=0).astype(jnp.bfloat16)
                weight_ref[g, base + r * width : base + (r + SUBLANES) * width, :] = block
        return carry

    lax.fori_loop(0, groups, one, 0, unroll=4)


def product(x, weight):
    high = x.astype(jnp.bfloat16)
    low = (x - high.astype(jnp.float32)).astype(jnp.bfloat16)
    left = jnp.concatenate(
        [jnp.concatenate([part, part], axis=1) for part in (high, low)], axis=0
    )
    both = jnp.dot(left, weight, preferred_element_type=jnp.float32)
    return both[: x.shape[0]] + both[x.shape[0] :]


def line_step(change, source_ref, target_ref, weight_ref, reach_ref, position):
    groups = source_ref.shape[0]

    def some(block, carry):
        new = []
        for j in range(WIDE):
            g = block * WIDE + j
            x = target_ref[g] - product(change(source_ref[g]), weight_ref[g])
            new.append(jnp.where(position < reach_ref[g, 0:1, :], x, 0.0))
        for j in range(WIDE):
            target_ref[block * WIDE + j] = new[j]
        return carry

    lax.fori_loop(0, groups // WIDE, some, 0)


def segment_steps(position, live):
    segments = position.shape[0]

    def back(x):
        return x - jnp.where(position == 0, 0.0, pltpu.roll(x, 1, 0))

    def forth(x):
        return jnp.where(position == segments - 1, 0.0, pltpu.roll(x, segments - 1, 0)) - x

    return back, forth


def current_sums(dots, sums, drive, position, live, starts):
    back, forth = segment_steps(position, live)
    amps, volts = list(dots[:3]), list(dots[3:])
    starts = [jnp.where(position == 0, x, 0.0) for x in starts]
    pull = [s * drive for s in sums]
    amps = [live * (a - forth(v) + p) for a, v, p in zip(amps, volts, pull)]
    volts = [live * (volts[i] - back(amps[i + 1]) + starts[i]) for i in range(2)]
    amps = [live * (amps[i] - forth(volts[i]) + pull[i]) for i in range(2)]
    volts = live * (volts[0] - back(amps[1]) + starts[2])
    return live * (amps[0] - forth(volts) + pull[0])


def responses(drive, position, live):
    back, forth = segment_steps(position, live)
    p1 = live * drive
    q1 = live * back(p1)
    p2 = live * forth(q1)
    q2 = live * back(p2)
    p3 = live * forth(q2)
    return p1, p2, p3, q1, q2, live * back(p3)


def partial_edge(field, magnetic, layer, part):
    ny = field.shape[2]
    for first in range(0, ny, SUBLANES):
        rows = pl.ds(first, SUBLANES)
        ex, ey, ez = (field[k, layer, rows, :] for k in range(3))
        if first + SUBLANES < ny:
            dy_ex = field[0, layer, pl.ds(first + 1, SUBLANES), :] - ex
        else:
            dy_ex = ahead(ex, 0)
        part[0, rows, :] = magnetic[1, layer, rows, :] - COURANT * (ahead(ex, 1) + ez)
        part[1, rows, :] = magnetic[2, layer, rows, :] + COURANT * (ey + dy_ex)


def magnetic_layer(field, magnetic, fresh, layer, following):
    ny = field.shape[2]
    for first in range(0, ny, SUBLANES):
        rows = pl.ds(first, SUBLANES)
        ex, ey, ez = (field[k, layer, rows, :] for k in range(3))
        if first + SUBLANES < ny:
            after = pl.ds(first + 1, SUBLANES)
            dy_ez = field[2, layer, after, :] - ez
            dy_ex = field[0, layer, after, :] - ex
        else:
            dy_ez, dy_ex = ahead(ez, 0), ahead(ex, 0)
        dx_ez = field[2, following, rows, :] - ez
        dx_ey = field[1, following, rows, :] - ey
        fresh[0, layer, rows, :] = magnetic[0, layer, rows, :] - COURANT * (dy_ez - ahead(ey, 1))
        fresh[1, layer, rows, :] = magnetic[1, layer, rows, :] - COURANT * (ahead(ex, 1) - dx_ez)
        fresh[2, layer, rows, :] = magnetic[2, layer, rows, :] - COURANT * (dx_ey - dy_ex)


def field_layer(field, magnetic, sigma, fresh, layer, hy_before, hz_before):
    ny, nz = field.shape[2:]
    top = lax.broadcasted_iota(jnp.int32, (SUBLANES, nz), 0) == 0
    before = [jnp.zeros((SUBLANES, nz), jnp.float32)] * 2

    def behind_rows(x, rolled_before):
        rolled = pltpu.roll(x, 1, 0)
        return x - jnp.where(top, rolled_before, rolled), rolled

    for first in range(0, ny, SUBLANES):
        rows = pl.ds(first, SUBLANES)
        ex, ey, ez = (field[k, layer, rows, :] for k in range(3))
        if first + SUBLANES < ny:
            after = pl.ds(first + 1, SUBLANES)
            dy_ez = field[2, layer, after, :] - ez
            dy_ex = field[0, layer, after, :] - ex
        else:
            dy_ez, dy_ex = ahead(ez, 0), ahead(ex, 0)
        dx_ez = field[2, layer + 1, rows, :] - ez
        dx_ey = field[1, layer + 1, rows, :] - ey
        hx = magnetic[0, layer, rows, :] - COURANT * (dy_ez - ahead(ey, 1))
        hy = magnetic[1, layer, rows, :] - COURANT * (ahead(ex, 1) - dx_ez)
        hz = magnetic[2, layer, rows, :] - COURANT * (dx_ey - dy_ex)
        for k, h in enumerate((hx, hy, hz)):
            fresh[k, layer, rows, :] = h
        dy_hx, before[0] = behind_rows(hx, before[0])
        dy_hz, before[1] = behind_rows(hz, before[1])
        curls = [
            dy_hz - behind(hy, 1),
            behind(hx, 1) - (hz - hz_before(rows)),
            (hy - hy_before(rows)) - dy_hx,
        ]
        conductivity = sigma[layer, rows, :]
        inverse = 1.0 / (1.0 + conductivity)
        keep = (1.0 - conductivity) * inverse
        factor = COURANT * inverse
        sigma[layer, rows, :] = factor
        for k, (old, curl) in enumerate(zip((ex, ey, ez), curls)):
            field[k, layer, rows, :] = keep * old + factor * curl


def opening_kernel(
    mesh_shape, cell_hbm, tangent_hbm, electric_hbm, magnetic_hbm, conductivity_hbm,
    volts_hbm, amps_hbm, inductance_hbm, capacitance_hbm, length_hbm, link_hbm,
    cell_ref, tangent_ref, induced_out, field, sigma, fresh, below_ref, volts_out, amps_out,
    length_ref, link_ref, reach_ref, inductance_weight, capacitance_weight,
    twice_ref, volts_state, amps_state, magnetic, volts_ref, amps_ref, inductance_ref, capacitance_ref,
    work_ref, flat_ref, send_ref, recv_ref, send_back_ref, recv_back_ref, part_ref,
    drive_ref, fixed_ref, even_ref, sent_ref, fixed_fed_ref, ends_ref, dot_ref, last_end_ref,
    last_fed_ref, amps_shift_ref, volts_shift_ref, response_ref,
    load_sem, row_sem, back_sem, edge_sem, feed_sem,
):
    depth, ny, nz = magnetic.shape[1:]
    count, me, partner = everyone(mesh_shape)
    cables = mesh_shape[1]

    def load(i, src, dst):
        copy = pltpu.make_async_copy(src, dst, load_sem.at[i])
        copy.start()
        return copy.wait

    cells_loaded, tangent_loaded = load(0, cell_hbm, cell_ref), load(1, tangent_hbm, tangent_ref)
    base = 2 + depth

    def layer_copy(i):
        return pltpu.make_async_copy(electric_hbm.at[:, i], field.at[:, i], load_sem.at[2 + i])

    for i in range(depth):
        layer_copy(i).start()
    lines = [
        load(base + i, src, dst)
        for i, (src, dst) in enumerate([
            (length_hbm, length_ref), (link_hbm, link_ref), (inductance_hbm, inductance_ref),
            (capacitance_hbm, capacitance_ref), (volts_hbm, volts_ref), (amps_hbm, amps_ref),
        ])
    ]
    last_layer = depth - 1
    magnetic_top = load(
        base + 6, magnetic_hbm.at[:, last_layer], magnetic.at[:, last_layer]
    )
    greeted = greet_all(count, partner)
    conductors, segments = volts_ref.shape[:2]
    halves = nz // LANES
    trays = cell_ref.shape[0] // halves
    groups = trays // SUBLANES
    chunks = ny // SUBLANES
    cells_loaded()

    def sample(layer, found):
        layer_copy(layer).wait()
        found = list(found)
        for half in range(halves):
            spots = []
            for group in range(groups):
                start = group * SUBLANES * halves + half
                cells = cell_ref[pl.ds(start, SUBLANES, stride=halves), :]
                spots.append((cells & (SUBLANES - 1), (cells >> 3) - layer * chunks))
            for chunk in range(chunks):
                rows = slice(chunk * SUBLANES, (chunk + 1) * SUBLANES)
                tiles = [
                    field[k, layer, rows, half * LANES : (half + 1) * LANES] for k in range(3)
                ]
                for group, (low, high) in enumerate(spots):
                    hit = high == chunk
                    for k in range(3):
                        at = (half * groups + group) * 3 + k
                        value = jnp.take_along_axis(tiles[k], low, axis=0)
                        found[at] = jnp.where(hit, value, found[at])
        return tuple(found)

    nothing = (jnp.zeros((SUBLANES, LANES), jnp.float32),) * (3 * halves * groups)
    found = lax.fori_loop(0, depth, sample, nothing)
    tangent_loaded()
    for half in range(halves):
        for group in range(groups):
            where = pl.ds(group * SUBLANES * halves + half, SUBLANES, stride=halves)
            at = (half * groups + group) * 3
            x, y, z = found[at : at + 3]
            flat_ref[where, :] = (
                tangent_ref[0, where, :] * x
                + tangent_ref[1, where, :] * y
                + tangent_ref[2, where, :] * z
            )
    for row in range(count):
        source = row // cables * cables + (row % cables + cables - 1) % cables
        send_ref[row, 0:1] = flat_ref[row : row + 1, :]
        send_ref[row, 1:2] = flat_ref[source : source + 1, :]
    start_rows, rows_here, rows_sent = row_exchange(
        count, me, partner, send_ref, recv_ref, row_sem
    )
    rest = pl.ds(0, last_layer)
    magnetic_rest = load(base + 7, magnetic_hbm.at[:, rest], magnetic.at[:, rest])
    sigma_loaded = load(base + 8, conductivity_hbm, sigma)
    greeted()
    start_rows()
    recv_ref[me] = send_ref[me]

    magnetic_top()
    partial_edge(field, magnetic, last_layer, part_ref)

    def complete():
        for first in range(0, ny, SUBLANES):
            rows = pl.ds(first, SUBLANES)
            below_ref[0, rows, :] = below_ref[0, rows, :] + COURANT * field[2, 0, rows, :]
            below_ref[1, rows, :] = below_ref[1, rows, :] - COURANT * field[1, 0, rows, :]

    band = ny // BANDS
    bands = []
    for i in range(BANDS):
        rows = pl.ds(i * band, band)
        sem = [edge_sem.at[4 * i + j] for j in range(4)]
        bands.append((
            edge_copy(
                mesh_shape, -1, field.at[pl.ds(1, 2), 0, rows], field.at[pl.ds(1, 2), depth, rows],
                *sem[:2],
            ),
            edge_copy(mesh_shape, 1, part_ref.at[:, rows], below_ref.at[:, rows], *sem[2:]),
        ))

    def edges(part, which=(0, 1), chosen=range(BANDS)):
        for i in chosen:
            for j in which:
                bands[i][j][part]()
    edges(0, chosen=range(EARLY_BANDS))
    for wait in lines:
        wait()
    position, live, last = line_positions(length_ref, segments)
    beyond = (position == length_ref[...]).astype(jnp.float32)
    before_last = (position == length_ref[...] - 2).astype(jnp.float32)
    spread = inductance_ref[0]
    for d in range(1, conductors):
        spread = spread + inductance_ref[d]
    fixed_ref[0] = spread
    for i in range(2):
        even_ref[i] = apply_symmetric(capacitance_ref, fixed_ref[i])
        fixed_ref[i + 1] = apply_symmetric(inductance_ref, even_ref[i])
    even_ref[2] = apply_symmetric(capacitance_ref, fixed_ref[2])
    sent_ref[0, 0:1] = length_ref[...].astype(jnp.float32)
    sent_ref[1] = fixed_ref[0]
    sent_ref[2] = fixed_ref[1]
    last_end_ref[1] = fixed_ref[2]

    def gather_ends(c, carry):
        row = pl.ds(c, 1)
        volts, amps = volts_ref[c], amps_ref[c]
        picks = (
            volts * beyond, volts * last, volts * before_last, amps * last, amps * before_last
        )
        for i, x in enumerate(picks):
            ends_ref[i, row, :] = jnp.sum(x, axis=0, keepdims=True)
        terms = [amps]
        terms += [even_ref[i, row, :] * amps for i in range(2)]
        terms += [fixed_ref[i, row, :] * volts for i in range(3)]
        return tuple(x + y for x, y in zip(carry, terms))

    zero = jnp.zeros((segments, LANES), jnp.float32)
    dots = lax.fori_loop(0, conductors, gather_ends, (zero,) * 6, unroll=2)
    for i, x in enumerate(dots):
        dot_ref[i] = x
    at_last, at_before = ends_ref[1], ends_ref[2]
    amps_last = ends_ref[3] - apply_symmetric(inductance_ref, ends_ref[0] - at_last)
    amps_before = ends_ref[4] - apply_symmetric(inductance_ref, at_last - at_before)
    volts_last = at_last - apply_symmetric(capacitance_ref, amps_last - amps_before)
    sent_ref[3] = amps_last
    sent_ref[4] = amps_last + apply_symmetric(inductance_ref, volts_last)

    fed_device = (lax.axis_index("slab"), (lax.axis_index("cable") + 1) % cables)
    fixed_feed, last_feed = [
        pltpu.make_async_remote_copy(
            src_ref=src, dst_ref=dst, send_sem=feed_sem.at[2 * i], recv_sem=feed_sem.at[2 * i + 1],
            device_id=fed_device, device_id_type=pl.DeviceIdType.MESH,
        )
        for i, (src, dst) in enumerate(
            [(sent_ref, fixed_fed_ref), (last_end_ref, last_fed_ref)]
        )
    ]
    fixed_feed.start()
    edges(0, chosen=range(EARLY_BANDS, BANDS))


    by_group(inductance_ref, work_ref)
    spread_weights(work_ref, twice_ref, inductance_weight)
    by_group(capacitance_ref, work_ref)
    spread_weights(work_ref, twice_ref, capacitance_weight)
    by_group(volts_ref, volts_state)
    by_group(amps_ref, amps_state)
    width = LANES // conductors
    lane = lax.broadcasted_iota(jnp.int32, (SUBLANES, LANES), 1) % width
    lengths = jnp.broadcast_to(length_ref[...], (SUBLANES, LANES))
    for g in range(conductors):
        reach_ref[g] = jnp.take_along_axis(lengths, lane + g * width, axis=1)
    back, forth = segment_steps(position, live)

    def amps_step():
        line_step(forth, volts_state, amps_state, inductance_weight, reach_ref, position)

    def volts_step():
        line_step(back, amps_state, volts_state, capacitance_weight, reach_ref, position)

    amps_step()
    volts_step()
    link = link_ref[...]
    sums = [jnp.sum(fixed_ref[i], axis=0, keepdims=True) for i in range(3)]
    fixed_feed.wait()
    fed1, fed3, first, second = (feed(fixed_fed_ref[i], link) for i in range(1, 5))
    fed_length = fixed_fed_ref[0, 0:1].astype(jnp.int32)
    fed_live = (position < fed_length).astype(jnp.float32)
    fed_last = (position == fed_length - 1).astype(jnp.float32)

    rows_here()
    for row in range(count):
        drive_ref[0, row : row + 1, :] = recv_ref[row, 0:1]
        drive_ref[1, row : row + 1, :] = recv_ref[row, 1:2]
    e1, e2, e3 = (
        feed(jnp.broadcast_to(jnp.sum(p * fed_last, axis=0, keepdims=True), link_rows), link)
        for link_rows in [(SUBLANES, LANES)]
        for p in responses(drive_ref[1], position, fed_live)[:3]
    )
    e1, e2, e3 = e1[0:1], e2[0:1], e3[0:1]
    first = first + fed1 * e1
    second = second + 2.0 * fed1 * e1 + fed3 * e2
    flat_ref[...] = current_sums(
        [dot_ref[i] for i in range(6)], sums, drive_ref[0], position, live,
        [jnp.sum(x * y, axis=0, keepdims=True)
         for x, y in ((even_ref[0], first), (even_ref[1], first), (even_ref[0], second))],
    ) / conductors
    for row in range(count):
        send_back_ref[row] = flat_ref[row : row + 1, :]
    start_back, back_here, back_sent = row_exchange(
        count, me, partner, send_back_ref, recv_back_ref, back_sem
    )
    start_back()
    recv_back_ref[me] = flat_ref[pl.ds(me, 1), :]

    p1, p2, p3, q1, q2, q3 = responses(drive_ref[0], position, live)
    for i, x in enumerate((3.0 * p1, 4.0 * p2, p3, 6.0 * q1, 5.0 * q2, q3)):
        response_ref[i] = x
    amps_step()
    volts_step()
    amps_step()
    by_conductor(amps_state, amps_out)

    def ending(c, carry):
        end = jnp.sum(amps_out[c] * last, axis=0, keepdims=True)
        last_end_ref[0, pl.ds(c, 1), :] = end
        return carry

    lax.fori_loop(0, conductors, ending, 0, unroll=4)
    last_feed.start()
    volts_step()
    by_conductor(volts_state, volts_out)
    magnetic_rest()

    sigma_loaded()
    magnetic_layer(field, magnetic, fresh, 0, 1)

    def inner(layer, carry):
        field_layer(
            field, magnetic, sigma, fresh, layer,
            lambda rows: fresh[1, layer - 1, rows, :], lambda rows: fresh[2, layer - 1, rows, :],
        )
        return carry

    lax.fori_loop(1, last_layer, inner, 0)
    last_feed.wait()
    third = (
        feed(last_fed_ref[0], link) + 3.0 * fed1 * e1 + 4.0 * fed3 * e2
        + feed(last_fed_ref[1], link) * e3
    )
    junction(
        first, second, third, inductance_ref, capacitance_ref, amps_shift_ref, volts_shift_ref
    )

    at = [position == i for i in range(3)]

    def settle(d, carry):
        row = pl.ds(d, 1)
        amps = amps_out[d]
        for i in range(2):
            amps = amps + jnp.where(at[i], amps_shift_ref[i, row, :], 0.0)
        volts = volts_out[d]
        for i in range(3):
            volts = volts + jnp.where(at[i], volts_shift_ref[i, row, :], 0.0)
        for i in range(3):
            amps = amps + fixed_ref[i, row, :] * response_ref[i]
            volts = volts - even_ref[i, row, :] * response_ref[3 + i]
        amps_out[d] = amps
        volts_out[d] = volts
        return carry

    lax.fori_loop(0, conductors, settle, 0, unroll=2)
    edges(1, (0,))
    magnetic_layer(field, magnetic, fresh, last_layer, depth)
    edges(1, (1,))

    @pl.when(me > 0)
    def _():
        complete()

    edges(2)
    rows_sent()
    back_sent()
    back_here()
    for row in range(count):
        induced_out[row : row + 1, :] = recv_back_ref[row]


def opening(
    mesh_shape, cells, steer, electric, magnetic, conductivity, volts, amps, inductance,
    capacitance, length, link,
):
    _, depth, ny, nz = electric.shape
    count = mesh_shape[0] * mesh_shape[1]
    conductors, segments, tubes = volts.shape
    assert cells.shape[0] == count and segments == count and tubes == LANES
    assert LANES % conductors == 0 and SUBLANES % (LANES // conductors) == 0
    hbm = pl.BlockSpec(memory_space=pl.ANY)
    lines = volts.shape
    matrix = inductance.shape
    edge = (2, ny, nz)
    end = (conductors, tubes)
    rows = (segments, tubes)
    groups = LANES // (LANES // conductors)
    weight = (groups, 2 * LANES, LANES)
    assert groups == conductors
    scratch = [
        (length.shape, jnp.int32), (link.shape, jnp.int32),
        ((groups, SUBLANES, LANES), jnp.int32), (weight, jnp.bfloat16), (weight, jnp.bfloat16),
    ]
    scratch += [
        (shape, jnp.float32)
        for shape in [
            (4, 2 * conductors, LANES), lines, lines, magnetic.shape, lines, lines, matrix, matrix,
            matrix, rows, (count, 2, LANES), (count, 2, LANES), (count, 1, LANES),
            (count, 1, LANES), edge,
            (2,) + rows, (3,) + end, (3,) + end, (5,) + end, (5,) + end, (5,) + end, (6,) + rows,
            (2,) + end, (2,) + end, (2,) + end, (3,) + end, (6,) + rows,
        ]
    ]
    outs = [
        (cells.shape, jnp.int32), (steer.shape, jnp.float32), (rows, jnp.float32),
        ((3, depth + 1, ny, nz), jnp.float32), (conductivity.shape, jnp.float32),
        (magnetic.shape, jnp.float32), (edge, jnp.float32), (lines, jnp.float32),
        (lines, jnp.float32),
    ]
    semaphores = [depth + 11, 2, 2, 4 * BANDS, 4]
    return pl.pallas_call(
        functools.partial(opening_kernel, mesh_shape),
        out_shape=[pltpu.VMEM(*out) for out in outs],
        in_specs=[hbm] * 11,
        out_specs=[pl.BlockSpec(memory_space=pltpu.VMEM)] * len(outs),
        scratch_shapes=[pltpu.VMEM(*kind) for kind in scratch]
        + [pltpu.SemaphoreType.DMA((number,)) for number in semaphores],
        compiler_params=pltpu.CompilerParams(
            collective_id=0, has_side_effects=True, vmem_limit_bytes=OPENING_VMEM
        ),
        name="lines_and_exchange",
    )(
        *(
            pltpu.with_memory_space_constraint(x, pltpu.HBM)
            for x in (
                cells, steer, electric, magnetic, conductivity, volts, amps, inductance,
                capacitance, length, link,
            )
        )
    )


def whole_base(fresh, old, conductivity, layer, first, hy_before, hz_before):
    rows = pl.ds(first, SUBLANES)
    hx, hy, hz = (fresh[k, layer, rows, :] for k in range(3))
    if first > 0:
        prior = pl.ds(first - 1, SUBLANES)
        dy_hz = hz - fresh[2, layer, prior, :]
        dy_hx = hx - fresh[0, layer, prior, :]
    else:
        dy_hz, dy_hx = behind(hz, 0), behind(hx, 0)
    curls = [
        dy_hz - behind(hy, 1),
        behind(hx, 1) - (hz - hz_before[rows, :]),
        (hy - hy_before[rows, :]) - dy_hx,
    ]
    inverse = 1.0 / (1.0 + conductivity)
    keep = (1.0 - conductivity) * inverse
    factor = COURANT * inverse
    return [keep * e + factor * curl for e, curl in zip(old, curls)], factor


def electric_kernel(
    cell_ref, tangent_ref, induced_ref, field, sigma, fresh, below_ref, volts_ref, amps_ref,
    electric_hbm, magnetic_hbm, volts_hbm, amps_hbm,
    new_ref, word_ref, merged_ref, copy_sem,
):
    _, depth, ny, nz = new_ref.shape
    halves = nz // LANES
    trays = cell_ref.shape[0] // halves
    groups = trays // SUBLANES
    chunks = ny // SUBLANES
    copies = [
        pltpu.make_async_copy(src, dst, copy_sem.at[depth + i])
        for i, (src, dst) in enumerate(
            [(fresh, magnetic_hbm), (amps_ref, amps_hbm), (volts_ref, volts_hbm)]
        )
    ]
    for copy in copies:
        copy.start()
    kept = []
    for half in range(halves):
        where = pl.ds(half, trays, stride=halves)
        cells = cell_ref[where, :]
        weights = [tangent_ref[k, where, :] * induced_ref[where, :] for k in range(3)]
        sums = [jnp.zeros_like(w) for w in weights]
        order = lax.broadcasted_iota(jnp.int32, cells.shape, 0)
        late = jnp.zeros(cells.shape, jnp.int32)
        for tray in range(trays):
            same = cells == cells[tray : tray + 1]
            late = jnp.where(same & (order > tray), 1, late)
            for k in range(3):
                sums[k] = sums[k] + jnp.where(same, weights[k][tray : tray + 1], 0.0)
        for k in range(3):
            merged_ref[k, half] = sums[k]
        block = jnp.where(late == 0, cells >> 3, -1)
        code = jnp.left_shift((order & (SUBLANES - 1)) | SUBLANES, (cells & (SUBLANES - 1)) * 4)
        kept.append((block, code))

    shift = 28 - 4 * lax.broadcasted_iota(jnp.int32, (SUBLANES, LANES), 0)

    def write(layer):
        return pltpu.make_async_copy(
            new_ref.at[:, layer], electric_hbm.at[:, layer], copy_sem.at[layer]
        )

    def one_layer(layer, before=None):
        here = lax.broadcasted_iota(jnp.int32, (chunks, LANES), 0) + layer * chunks
        for half in range(halves):
            block, code = kept[half]
            for group in range(groups):
                word = jnp.zeros((chunks, LANES), jnp.int32)
                for tray in range(group * SUBLANES, (group + 1) * SUBLANES):
                    hit = block[tray : tray + 1] == here
                    word = word | jnp.where(hit, code[tray : tray + 1], 0)
                word_ref[half, group] = word
        for chunk in range(chunks):
            first = chunk * SUBLANES
            rows = pl.ds(first, SUBLANES)
            bases, factor = [field[k, layer, rows, :] for k in range(3)], sigma[layer, rows, :]
            if before is not None:
                bases, factor = whole_base(fresh, bases, factor, layer, first, *before)
            deposits = [[None] * halves for _ in range(3)]
            for half in range(halves):
                picks = []
                for group in range(groups):
                    word = word_ref[half, group, chunk : chunk + 1, :]
                    word = jnp.left_shift(jnp.broadcast_to(word, (SUBLANES, LANES)), shift)
                    low = lax.shift_right_logical(word, 28) & (SUBLANES - 1)
                    picks.append((word < 0, low))
                for k in range(3):
                    deposit = jnp.zeros((SUBLANES, LANES), jnp.float32)
                    for group, (hit, low) in enumerate(picks):
                        part = merged_ref[k, half, group * SUBLANES : (group + 1) * SUBLANES, :]
                        deposit = jnp.where(
                            hit, jnp.take_along_axis(part, low, axis=0), deposit
                        )
                    deposits[k][half] = deposit
            for k in range(3):
                deposit = jnp.concatenate(deposits[k], axis=1)
                new_ref[k, layer, rows, :] = bases[k] - factor * deposit
        write(layer).start()

    def inner(layer, carry):
        one_layer(layer)
        return carry

    lax.fori_loop(1, depth - 1, inner, 0)
    one_layer(0, (below_ref.at[0], below_ref.at[1]))
    one_layer(depth - 1, (fresh.at[1, depth - 2], fresh.at[2, depth - 2]))
    for layer in range(depth):
        write(layer).wait()
    for copy in copies:
        copy.wait()


def field_step(*handed):
    cells, fresh, volts, amps = handed[0], handed[5], handed[7], handed[8]
    _, depth, ny, nz = fresh.shape
    halves = nz // LANES
    trays = cells.shape[0] // halves
    vmem = pl.BlockSpec(memory_space=pltpu.VMEM)
    hbm = pl.BlockSpec(memory_space=pl.ANY)
    shapes = [fresh.shape, fresh.shape, volts.shape, amps.shape]
    return pl.pallas_call(
        electric_kernel,
        out_shape=[jax.ShapeDtypeStruct(shape, jnp.float32) for shape in shapes],
        in_specs=[vmem] * len(handed),
        out_specs=[hbm] * len(shapes),
        scratch_shapes=[
            pltpu.VMEM(fresh.shape, jnp.float32),
            pltpu.VMEM((halves, trays // SUBLANES, ny // SUBLANES, LANES), jnp.int32),
            pltpu.VMEM((3, halves, trays, LANES), jnp.float32),
            pltpu.SemaphoreType.DMA((depth + 3,)),
        ],
        compiler_params=pltpu.CompilerParams(vmem_limit_bytes=CLOSING_VMEM),
        name="field_step",
    )(*handed)


def local(
    mesh_shape,
    electric,
    magnetic,
    conductivity,
    voltage,
    current,
    inverse_inductance,
    inverse_capacitance,
    tangent,
    sample_cell,
    tube_length,
    junction_link,
):
    cells = sample_cell.reshape(-1, LANES)
    steer = tangent.reshape(3, -1, LANES)
    handed = opening(
        mesh_shape, cells, steer, electric, magnetic, conductivity, voltage, current,
        inverse_inductance, inverse_capacitance, tube_length[None, :], junction_link[None, :],
    )
    return tuple(field_step(*handed))


def solution(mesh):
    mesh_shape = (mesh.shape["slab"], mesh.shape["cable"])
    return jax.shard_map(
        functools.partial(local, mesh_shape),
        mesh=mesh,
        in_specs=(
            P(None, AXES, None, None),
            P(None, AXES, None, None),
            P(AXES, None, None),
            P(None, None, AXES),
            P(None, None, AXES),
            P(None, None, AXES),
            P(None, None, AXES),
            P(None, AXES, None),
            P(AXES, None),
            P(AXES),
            P(AXES),
        ),
        out_specs=(
            P(None, AXES, None, None),
            P(None, AXES, None, None),
            P(None, None, AXES),
            P(None, None, AXES),
        ),
        check_vma=False,
    )
```

```python
import functools

import jax
import jax.numpy as jnp
from jax import lax
from jax.experimental import pallas as pl
from jax.experimental.pallas import tpu as pltpu
from jax.sharding import PartitionSpec as P

COURANT = 0.5
LANES = 128
SUBLANES = 8
AXES = ("slab", "cable")
OPENING_VMEM = 30 << 20
CLOSING_VMEM = 8 << 20
WIDE = 32
BANDS = 1
EARLY_BANDS = 0


def everyone(mesh_shape):
    slabs, cables = mesh_shape
    count = slabs * cables
    assert count & (count - 1) == 0
    me = lax.axis_index("slab") * cables + lax.axis_index("cable")

    def partner(step):
        peer = me ^ (count - step)
        return peer, (peer // cables, peer % cables)

    return count, me, partner


def greet_all(count, partner):
    barrier = pltpu.get_barrier_semaphore()

    def greet(step, carry):
        pl.semaphore_signal(
            barrier, inc=1, device_id=partner(step)[1], device_id_type=pl.DeviceIdType.MESH,
        )
        return carry

    lax.fori_loop(1, count, greet, 0)
    return lambda: pl.semaphore_wait(barrier, count - 1)


def row_exchange(count, me, partner, send_ref, recv_ref, sems):
    def copy(src, dst, place):
        return pltpu.make_async_remote_copy(
            src_ref=src, dst_ref=dst, send_sem=sems.at[0], recv_sem=sems.at[1],
            device_id=place, device_id_type=pl.DeviceIdType.MESH,
        )

    def start(step, carry):
        peer, place = partner(step)
        copy(send_ref.at[peer], recv_ref.at[me], place).start()
        return carry

    others = pl.ds(0, count - 1)
    every = copy(send_ref.at[others], recv_ref.at[others], partner(1)[1])

    return lambda: lax.fori_loop(1, count, start, 0), every.wait_recv, every.wait_send


def edge_copy(mesh_shape, by, src, dst, send_sem, recv_sem, settle=None):
    slabs, cables = mesh_shape
    count = slabs * cables
    me = lax.axis_index("slab") * cables + lax.axis_index("cable")
    has_target = (me + by >= 0) & (me + by < count)
    has_source = (me - by >= 0) & (me - by < count)
    target = (me + by + count) % count
    copy = pltpu.make_async_remote_copy(
        src_ref=src, dst_ref=dst, send_sem=send_sem, recv_sem=recv_sem,
        device_id=(target // cables, target % cables), device_id_type=pl.DeviceIdType.MESH,
    )

    def start():
        @pl.when(has_target)
        def _():
            copy.start()

    def received():
        @pl.when(has_source)
        def _():
            copy.wait_recv()
            if settle is not None:
                settle()

        @pl.when(jnp.logical_not(has_source))
        def _():
            dst[...] = jnp.zeros(dst.shape, jnp.float32)

    def sent():
        @pl.when(has_target)
        def _():
            copy.wait_send()

    return start, received, sent


def at_edge(rolled, axis, last):
    tile = LANES if axis == 1 else SUBLANES
    extent = rolled.shape[axis]
    if extent == tile:
        index = lax.broadcasted_iota(jnp.int32, rolled.shape, axis)
        return jnp.where(index == (tile - 1 if last else 0), 0.0, rolled)
    cut = extent - tile if last else tile
    first = lax.slice_in_dim(rolled, 0, cut, axis=axis)
    second = lax.slice_in_dim(rolled, cut, extent, axis=axis)
    edge = second if last else first
    index = lax.broadcasted_iota(jnp.int32, edge.shape, axis)
    edge = jnp.where(index == (tile - 1 if last else 0), 0.0, edge)
    return jnp.concatenate([first, edge] if last else [edge, second], axis=axis)


def ahead(x, axis):
    return at_edge(pltpu.roll(x, x.shape[axis] - 1, axis), axis, True) - x


def behind(x, axis):
    return x - at_edge(pltpu.roll(x, 1, axis), axis, False)


def line_positions(length_ref, segments):
    lanes = length_ref.shape[1]
    position = lax.broadcasted_iota(jnp.int32, (segments, lanes), 0)
    live = (position < length_ref[...]).astype(jnp.float32)
    last = (position == length_ref[...] - 1).astype(jnp.float32)
    return position, live, last


def feed(end, link):
    picked = []
    for start in range(0, end.shape[0], SUBLANES):
        rows = end[start : start + SUBLANES]
        picked.append(
            jnp.take_along_axis(rows, jnp.broadcast_to(link, rows.shape), axis=1)
        )
    return jnp.concatenate(picked, axis=0)


def apply_symmetric(matrix_ref, vector):
    sums = [None] * 4
    for d in range(vector.shape[0]):
        term = matrix_ref[d] * vector[d : d + 1]
        sums[d % 4] = term if sums[d % 4] is None else sums[d % 4] + term
    return (sums[0] + sums[1]) + (sums[2] + sums[3])


def junction(
    first, second, third, inductance_ref, capacitance_ref, amps_shift_ref, volts_shift_ref,
):
    volts0 = apply_symmetric(capacitance_ref, first)
    fed = apply_symmetric(capacitance_ref, second)
    amps0 = apply_symmetric(inductance_ref, volts0)
    spread = apply_symmetric(capacitance_ref, amps0)
    volts0 = volts0 - spread + fed
    volts1 = spread
    amps0 = amps0 + apply_symmetric(inductance_ref, volts0 - volts1)
    amps1 = apply_symmetric(inductance_ref, volts1)
    amps_shift_ref[0] = amps0
    amps_shift_ref[1] = amps1
    volts_shift_ref[0] = volts0 - apply_symmetric(capacitance_ref, amps0 - third)
    volts_shift_ref[1] = volts1 - apply_symmetric(capacitance_ref, amps1 - amps0)
    volts_shift_ref[2] = apply_symmetric(capacitance_ref, amps1)


def turn_pieces(tiles):
    number = len(tiles)
    piece = lax.broadcasted_iota(jnp.int32, (SUBLANES, LANES), 1) // (LANES // number)
    bit = 1
    while bit < number:
        odd = (piece & bit) != 0
        tiles = [jnp.where(odd, tiles[(i + bit) % number], tiles[i]) for i in range(number)]
        bit *= 2
    return [tiles[-i % number] for i in range(number)]


def by_group(src_ref, dst_ref):
    number, rows = src_ref.shape[:2]
    width = LANES // number

    def one(r, carry):
        here = pl.ds(pl.multiple_of(r * SUBLANES, SUBLANES), SUBLANES)
        tiles = [src_ref[0, here, :]]
        for i in range(1, number):
            tiles.append(pltpu.roll(src_ref[i, here, :], width * i, 1))
        for i, tile in enumerate(turn_pieces(tiles)):
            dst_ref[i, here, :] = tile
        return carry

    lax.fori_loop(0, rows // SUBLANES, one, 0, unroll=4)


def by_conductor(src_ref, dst_ref):
    number, rows = src_ref.shape[:2]
    width = LANES // number

    def one(r, carry):
        here = pl.ds(pl.multiple_of(r * SUBLANES, SUBLANES), SUBLANES)
        tiles = turn_pieces([src_ref[i, here, :] for i in range(number)])
        dst_ref[0, here, :] = tiles[0]
        for i in range(1, number):
            dst_ref[i, here, :] = pltpu.roll(tiles[i], LANES - width * i, 1)
        return carry

    lax.fori_loop(0, rows // SUBLANES, one, 0, unroll=4)


def spread_weights(src_ref, twice_ref, weight_ref):
    groups, conductors = src_ref.shape[:2]
    width = LANES // conductors
    lane = lax.broadcasted_iota(jnp.int32, (SUBLANES, LANES), 1)
    sub = lax.broadcasted_iota(jnp.int32, (SUBLANES, LANES), 0)
    diagonal = (lane % width) == (sub % width)
    source = [(j * SUBLANES + sub) // width for j in range(width)]

    def one(g, carry):
        slot = lax.rem(g, twice_ref.shape[0])
        for base in range(0, 2 * conductors, conductors):
            twice_ref[slot, base : base + conductors, :] = src_ref[g]
        for r in range(0, conductors, SUBLANES):
            x = twice_ref[slot, pl.ds(conductors - g + r, SUBLANES), :]
            high = x.astype(jnp.bfloat16).astype(jnp.float32)
            for base, part in ((0, high), (LANES, x - high)):
                rows = [
                    jnp.where(diagonal, jnp.take_along_axis(part, s, axis=0), 0.0) for s in source
                ]
                block = jnp.concatenate(rows, axis=0).astype(jnp.bfloat16)
                weight_ref[g, base + r * width : base + (r + SUBLANES) * width, :] = block
        return carry

    lax.fori_loop(0, groups, one, 0, unroll=4)


def product(x, weight):
    high = x.astype(jnp.bfloat16)
    low = (x - high.astype(jnp.float32)).astype(jnp.bfloat16)
    left = jnp.concatenate(
        [jnp.concatenate([part, part], axis=1) for part in (high, low)], axis=0
    )
    both = jnp.dot(left, weight, preferred_element_type=jnp.float32)
    return both[: x.shape[0]] + both[x.shape[0] :]


def line_step(change, source_ref, target_ref, weight_ref, reach_ref, position):
    groups = source_ref.shape[0]

    def some(block, carry):
        new = []
        for j in range(WIDE):
            g = block * WIDE + j
            x = target_ref[g] - product(change(source_ref[g]), weight_ref[g])
            new.append(jnp.where(position < reach_ref[g, 0:1, :], x, 0.0))
        for j in range(WIDE):
            target_ref[block * WIDE + j] = new[j]
        return carry

    lax.fori_loop(0, groups // WIDE, some, 0)


def segment_steps(position, live):
    segments = position.shape[0]

    def back(x):
        return x - jnp.where(position == 0, 0.0, pltpu.roll(x, 1, 0))

    def forth(x):
        return jnp.where(position == segments - 1, 0.0, pltpu.roll(x, segments - 1, 0)) - x

    return back, forth


def current_sums(dots, sums, drive, position, live, starts):
    back, forth = segment_steps(position, live)
    amps, volts = list(dots[:3]), list(dots[3:])
    starts = [jnp.where(position == 0, x, 0.0) for x in starts]
    pull = [s * drive for s in sums]
    amps = [live * (a - forth(v) + p) for a, v, p in zip(amps, volts, pull)]
    volts = [live * (volts[i] - back(amps[i + 1]) + starts[i]) for i in range(2)]
    amps = [live * (amps[i] - forth(volts[i]) + pull[i]) for i in range(2)]
    volts = live * (volts[0] - back(amps[1]) + starts[2])
    return live * (amps[0] - forth(volts) + pull[0])


def responses(drive, position, live):
    back, forth = segment_steps(position, live)
    p1 = live * drive
    q1 = live * back(p1)
    p2 = live * forth(q1)
    q2 = live * back(p2)
    p3 = live * forth(q2)
    return p1, p2, p3, q1, q2, live * back(p3)


def partial_edge(field, magnetic, layer, part):
    ny = field.shape[2]
    for first in range(0, ny, SUBLANES):
        rows = pl.ds(first, SUBLANES)
        ex, ey, ez = (field[k, layer, rows, :] for k in range(3))
        if first + SUBLANES < ny:
            dy_ex = field[0, layer, pl.ds(first + 1, SUBLANES), :] - ex
        else:
            dy_ex = ahead(ex, 0)
        part[0, rows, :] = magnetic[1, layer, rows, :] - COURANT * (ahead(ex, 1) + ez)
        part[1, rows, :] = magnetic[2, layer, rows, :] + COURANT * (ey + dy_ex)


def magnetic_layer(field, magnetic, fresh, layer, following):
    ny = field.shape[2]
    for first in range(0, ny, SUBLANES):
        rows = pl.ds(first, SUBLANES)
        ex, ey, ez = (field[k, layer, rows, :] for k in range(3))
        if first + SUBLANES < ny:
            after = pl.ds(first + 1, SUBLANES)
            dy_ez = field[2, layer, after, :] - ez
            dy_ex = field[0, layer, after, :] - ex
        else:
            dy_ez, dy_ex = ahead(ez, 0), ahead(ex, 0)
        dx_ez = field[2, following, rows, :] - ez
        dx_ey = field[1, following, rows, :] - ey
        fresh[0, layer, rows, :] = magnetic[0, layer, rows, :] - COURANT * (dy_ez - ahead(ey, 1))
        fresh[1, layer, rows, :] = magnetic[1, layer, rows, :] - COURANT * (ahead(ex, 1) - dx_ez)
        fresh[2, layer, rows, :] = magnetic[2, layer, rows, :] - COURANT * (dx_ey - dy_ex)


def field_layer(field, magnetic, sigma, fresh, layer, hy_before, hz_before):
    ny, nz = field.shape[2:]
    top = lax.broadcasted_iota(jnp.int32, (SUBLANES, nz), 0) == 0
    before = [jnp.zeros((SUBLANES, nz), jnp.float32)] * 2

    def behind_rows(x, rolled_before):
        rolled = pltpu.roll(x, 1, 0)
        return x - jnp.where(top, rolled_before, rolled), rolled

    for first in range(0, ny, SUBLANES):
        rows = pl.ds(first, SUBLANES)
        ex, ey, ez = (field[k, layer, rows, :] for k in range(3))
        if first + SUBLANES < ny:
            after = pl.ds(first + 1, SUBLANES)
            dy_ez = field[2, layer, after, :] - ez
            dy_ex = field[0, layer, after, :] - ex
        else:
            dy_ez, dy_ex = ahead(ez, 0), ahead(ex, 0)
        dx_ez = field[2, layer + 1, rows, :] - ez
        dx_ey = field[1, layer + 1, rows, :] - ey
        hx = magnetic[0, layer, rows, :] - COURANT * (dy_ez - ahead(ey, 1))
        hy = magnetic[1, layer, rows, :] - COURANT * (ahead(ex, 1) - dx_ez)
        hz = magnetic[2, layer, rows, :] - COURANT * (dx_ey - dy_ex)
        for k, h in enumerate((hx, hy, hz)):
            fresh[k, layer, rows, :] = h
        dy_hx, before[0] = behind_rows(hx, before[0])
        dy_hz, before[1] = behind_rows(hz, before[1])
        curls = [
            dy_hz - behind(hy, 1),
            behind(hx, 1) - (hz - hz_before(rows)),
            (hy - hy_before(rows)) - dy_hx,
        ]
        conductivity = sigma[layer, rows, :]
        inverse = 1.0 / (1.0 + conductivity)
        keep = (1.0 - conductivity) * inverse
        factor = COURANT * inverse
        sigma[layer, rows, :] = factor
        for k, (old, curl) in enumerate(zip((ex, ey, ez), curls)):
            field[k, layer, rows, :] = keep * old + factor * curl


def opening_kernel(
    mesh_shape, cell_hbm, tangent_hbm, electric_hbm, magnetic_hbm, conductivity_hbm,
    volts_hbm, amps_hbm, inductance_hbm, capacitance_hbm, length_hbm, link_hbm,
    cell_ref, tangent_ref, induced_out, field, sigma, fresh, below_ref, volts_out, amps_out,
    length_ref, link_ref, reach_ref, inductance_weight, capacitance_weight,
    twice_ref, volts_state, amps_state, magnetic, volts_ref, amps_ref, inductance_ref, capacitance_ref,
    work_ref, flat_ref, send_ref, recv_ref, send_back_ref, recv_back_ref, part_ref,
    drive_ref, fixed_ref, even_ref, sent_ref, fixed_fed_ref, ends_ref, dot_ref, last_end_ref,
    last_fed_ref, amps_shift_ref, volts_shift_ref, response_ref,
    load_sem, row_sem, back_sem, edge_sem, feed_sem,
):
    depth, ny, nz = magnetic.shape[1:]
    count, me, partner = everyone(mesh_shape)
    cables = mesh_shape[1]

    def load(i, src, dst):
        copy = pltpu.make_async_copy(src, dst, load_sem.at[i])
        copy.start()
        return copy.wait

    cells_loaded, tangent_loaded = load(0, cell_hbm, cell_ref), load(1, tangent_hbm, tangent_ref)
    base = 2 + depth

    def layer_copy(i):
        return pltpu.make_async_copy(electric_hbm.at[:, i], field.at[:, i], load_sem.at[2 + i])

    for i in range(depth):
        layer_copy(i).start()
    lines = [
        load(base + i, src, dst)
        for i, (src, dst) in enumerate([
            (length_hbm, length_ref), (link_hbm, link_ref), (inductance_hbm, inductance_ref),
            (capacitance_hbm, capacitance_ref), (volts_hbm, volts_ref), (amps_hbm, amps_ref),
        ])
    ]
    last_layer = depth - 1
    magnetic_top = load(
        base + 6, magnetic_hbm.at[:, last_layer], magnetic.at[:, last_layer]
    )
    greeted = greet_all(count, partner)
    conductors, segments = volts_ref.shape[:2]
    halves = nz // LANES
    trays = cell_ref.shape[0] // halves
    groups = trays // SUBLANES
    chunks = ny // SUBLANES
    cells_loaded()

    def sample(layer, found):
        layer_copy(layer).wait()
        found = list(found)
        for half in range(halves):
            spots = []
            for group in range(groups):
                start = group * SUBLANES * halves + half
                cells = cell_ref[pl.ds(start, SUBLANES, stride=halves), :]
                spots.append((cells & (SUBLANES - 1), (cells >> 3) - layer * chunks))
            for chunk in range(chunks):
                rows = slice(chunk * SUBLANES, (chunk + 1) * SUBLANES)
                tiles = [
                    field[k, layer, rows, half * LANES : (half + 1) * LANES] for k in range(3)
                ]
                for group, (low, high) in enumerate(spots):
                    hit = high == chunk
                    for k in range(3):
                        at = (half * groups + group) * 3 + k
                        value = jnp.take_along_axis(tiles[k], low, axis=0)
                        found[at] = jnp.where(hit, value, found[at])
        return tuple(found)

    nothing = (jnp.zeros((SUBLANES, LANES), jnp.float32),) * (3 * halves * groups)
    found = lax.fori_loop(0, depth, sample, nothing)
    tangent_loaded()
    for half in range(halves):
        for group in range(groups):
            where = pl.ds(group * SUBLANES * halves + half, SUBLANES, stride=halves)
            at = (half * groups + group) * 3
            x, y, z = found[at : at + 3]
            flat_ref[where, :] = (
                tangent_ref[0, where, :] * x
                + tangent_ref[1, where, :] * y
                + tangent_ref[2, where, :] * z
            )
    for row in range(count):
        source = row // cables * cables + (row % cables + cables - 1) % cables
        send_ref[row, 0:1] = flat_ref[row : row + 1, :]
        send_ref[row, 1:2] = flat_ref[source : source + 1, :]
    start_rows, rows_here, rows_sent = row_exchange(
        count, me, partner, send_ref, recv_ref, row_sem
    )
    rest = pl.ds(0, last_layer)
    magnetic_rest = load(base + 7, magnetic_hbm.at[:, rest], magnetic.at[:, rest])
    sigma_loaded = load(base + 8, conductivity_hbm, sigma)
    greeted()
    start_rows()
    recv_ref[me] = send_ref[me]

    magnetic_top()
    partial_edge(field, magnetic, last_layer, part_ref)

    def complete():
        for first in range(0, ny, SUBLANES):
            rows = pl.ds(first, SUBLANES)
            below_ref[0, rows, :] = below_ref[0, rows, :] + COURANT * field[2, 0, rows, :]
            below_ref[1, rows, :] = below_ref[1, rows, :] - COURANT * field[1, 0, rows, :]

    band = ny // BANDS
    bands = []
    for i in range(BANDS):
        rows = pl.ds(i * band, band)
        sem = [edge_sem.at[4 * i + j] for j in range(4)]
        bands.append((
            edge_copy(
                mesh_shape, -1, field.at[pl.ds(1, 2), 0, rows], field.at[pl.ds(1, 2), depth, rows],
                *sem[:2],
            ),
            edge_copy(mesh_shape, 1, part_ref.at[:, rows], below_ref.at[:, rows], *sem[2:]),
        ))

    def edges(part, which=(0, 1), chosen=range(BANDS)):
        for i in chosen:
            for j in which:
                bands[i][j][part]()
    edges(0, chosen=range(EARLY_BANDS))
    for wait in lines:
        wait()
    position, live, last = line_positions(length_ref, segments)
    beyond = (position == length_ref[...]).astype(jnp.float32)
    before_last = (position == length_ref[...] - 2).astype(jnp.float32)
    parts = [inductance_ref[d] for d in range(4)]
    for d in range(4, conductors):
        parts[d % 4] = parts[d % 4] + inductance_ref[d]
    fixed_ref[0] = (parts[0] + parts[1]) + (parts[2] + parts[3])
    for i in range(2):
        even_ref[i] = apply_symmetric(capacitance_ref, fixed_ref[i])
        fixed_ref[i + 1] = apply_symmetric(inductance_ref, even_ref[i])
    even_ref[2] = apply_symmetric(capacitance_ref, fixed_ref[2])
    sent_ref[0, 0:1] = length_ref[...].astype(jnp.float32)
    sent_ref[1] = fixed_ref[0]
    sent_ref[2] = fixed_ref[1]
    last_end_ref[1] = fixed_ref[2]

    def gather_ends(c, carry):
        row = pl.ds(c, 1)
        volts, amps = volts_ref[c], amps_ref[c]
        picks = (
            volts * beyond, volts * last, volts * before_last, amps * last, amps * before_last
        )
        for i, x in enumerate(picks):
            ends_ref[i, row, :] = jnp.sum(x, axis=0, keepdims=True)
        terms = [amps]
        terms += [even_ref[i, row, :] * amps for i in range(2)]
        terms += [fixed_ref[i, row, :] * volts for i in range(3)]
        return tuple(x + y for x, y in zip(carry, terms))

    zero = jnp.zeros((segments, LANES), jnp.float32)
    dots = lax.fori_loop(0, conductors, gather_ends, (zero,) * 6, unroll=8)
    for i, x in enumerate(dots):
        dot_ref[i] = x
    at_last, at_before = ends_ref[1], ends_ref[2]
    amps_last = ends_ref[3] - apply_symmetric(inductance_ref, ends_ref[0] - at_last)
    amps_before = ends_ref[4] - apply_symmetric(inductance_ref, at_last - at_before)
    volts_last = at_last - apply_symmetric(capacitance_ref, amps_last - amps_before)
    sent_ref[3] = amps_last
    sent_ref[4] = amps_last + apply_symmetric(inductance_ref, volts_last)

    fed_device = (lax.axis_index("slab"), (lax.axis_index("cable") + 1) % cables)
    fixed_feed, last_feed = [
        pltpu.make_async_remote_copy(
            src_ref=src, dst_ref=dst, send_sem=feed_sem.at[2 * i], recv_sem=feed_sem.at[2 * i + 1],
            device_id=fed_device, device_id_type=pl.DeviceIdType.MESH,
        )
        for i, (src, dst) in enumerate(
            [(sent_ref, fixed_fed_ref), (last_end_ref, last_fed_ref)]
        )
    ]
    fixed_feed.start()
    edges(0, chosen=range(EARLY_BANDS, BANDS))


    by_group(inductance_ref, work_ref)
    spread_weights(work_ref, twice_ref, inductance_weight)
    by_group(capacitance_ref, work_ref)
    spread_weights(work_ref, twice_ref, capacitance_weight)
    by_group(volts_ref, volts_state)
    by_group(amps_ref, amps_state)
    width = LANES // conductors
    lane = lax.broadcasted_iota(jnp.int32, (SUBLANES, LANES), 1) % width
    lengths = jnp.broadcast_to(length_ref[...], (SUBLANES, LANES))
    for g in range(conductors):
        reach_ref[g] = jnp.take_along_axis(lengths, lane + g * width, axis=1)
    back, forth = segment_steps(position, live)

    def amps_step():
        line_step(forth, volts_state, amps_state, inductance_weight, reach_ref, position)

    def volts_step():
        line_step(back, amps_state, volts_state, capacitance_weight, reach_ref, position)

    amps_step()
    volts_step()
    link = link_ref[...]
    sums = [jnp.sum(fixed_ref[i], axis=0, keepdims=True) for i in range(3)]
    fixed_feed.wait()
    fed1, fed3, first, second = (feed(fixed_fed_ref[i], link) for i in range(1, 5))
    fed_length = fixed_fed_ref[0, 0:1].astype(jnp.int32)
    fed_live = (position < fed_length).astype(jnp.float32)
    fed_last = (position == fed_length - 1).astype(jnp.float32)

    rows_here()
    for row in range(count):
        drive_ref[0, row : row + 1, :] = recv_ref[row, 0:1]
        drive_ref[1, row : row + 1, :] = recv_ref[row, 1:2]
    e1, e2, e3 = (
        feed(jnp.broadcast_to(jnp.sum(p * fed_last, axis=0, keepdims=True), link_rows), link)
        for link_rows in [(SUBLANES, LANES)]
        for p in responses(drive_ref[1], position, fed_live)[:3]
    )
    e1, e2, e3 = e1[0:1], e2[0:1], e3[0:1]
    first = first + fed1 * e1
    second = second + 2.0 * fed1 * e1 + fed3 * e2
    flat_ref[...] = current_sums(
        [dot_ref[i] for i in range(6)], sums, drive_ref[0], position, live,
        [jnp.sum(x * y, axis=0, keepdims=True)
         for x, y in ((even_ref[0], first), (even_ref[1], first), (even_ref[0], second))],
    ) / conductors
    for row in range(count):
        send_back_ref[row] = flat_ref[row : row + 1, :]
    start_back, back_here, back_sent = row_exchange(
        count, me, partner, send_back_ref, recv_back_ref, back_sem
    )
    start_back()
    recv_back_ref[me] = flat_ref[pl.ds(me, 1), :]

    p1, p2, p3, q1, q2, q3 = responses(drive_ref[0], position, live)
    for i, x in enumerate((3.0 * p1, 4.0 * p2, p3, 6.0 * q1, 5.0 * q2, q3)):
        response_ref[i] = x
    amps_step()
    volts_step()
    amps_step()
    by_conductor(amps_state, amps_out)

    def ending(c, carry):
        end = jnp.sum(amps_out[c] * last, axis=0, keepdims=True)
        last_end_ref[0, pl.ds(c, 1), :] = end
        return carry

    lax.fori_loop(0, conductors, ending, 0, unroll=4)
    last_feed.start()
    volts_step()
    by_conductor(volts_state, volts_out)
    magnetic_rest()

    sigma_loaded()
    magnetic_layer(field, magnetic, fresh, 0, 1)

    def inner(layer, carry):
        field_layer(
            field, magnetic, sigma, fresh, layer,
            lambda rows: fresh[1, layer - 1, rows, :], lambda rows: fresh[2, layer - 1, rows, :],
        )
        return carry

    lax.fori_loop(1, last_layer, inner, 0)
    last_feed.wait()
    third = (
        feed(last_fed_ref[0], link) + 3.0 * fed1 * e1 + 4.0 * fed3 * e2
        + feed(last_fed_ref[1], link) * e3
    )
    junction(
        first, second, third, inductance_ref, capacitance_ref, amps_shift_ref, volts_shift_ref
    )

    at = [position == i for i in range(3)]

    def settle(d, carry):
        row = pl.ds(d, 1)
        amps = amps_out[d]
        for i in range(2):
            amps = amps + jnp.where(at[i], amps_shift_ref[i, row, :], 0.0)
        volts = volts_out[d]
        for i in range(3):
            volts = volts + jnp.where(at[i], volts_shift_ref[i, row, :], 0.0)
        for i in range(3):
            amps = amps + fixed_ref[i, row, :] * response_ref[i]
            volts = volts - even_ref[i, row, :] * response_ref[3 + i]
        amps_out[d] = amps
        volts_out[d] = volts
        return carry

    lax.fori_loop(0, conductors, settle, 0, unroll=2)
    edges(1, (0,))
    magnetic_layer(field, magnetic, fresh, last_layer, depth)
    edges(1, (1,))

    @pl.when(me > 0)
    def _():
        complete()

    edges(2)
    rows_sent()
    back_sent()
    back_here()
    for row in range(count):
        induced_out[row : row + 1, :] = recv_back_ref[row]


def opening(
    mesh_shape, cells, steer, electric, magnetic, conductivity, volts, amps, inductance,
    capacitance, length, link,
):
    _, depth, ny, nz = electric.shape
    count = mesh_shape[0] * mesh_shape[1]
    conductors, segments, tubes = volts.shape
    assert cells.shape[0] == count and segments == count and tubes == LANES
    assert LANES % conductors == 0 and SUBLANES % (LANES // conductors) == 0
    hbm = pl.BlockSpec(memory_space=pl.ANY)
    lines = volts.shape
    matrix = inductance.shape
    edge = (2, ny, nz)
    end = (conductors, tubes)
    rows = (segments, tubes)
    groups = LANES // (LANES // conductors)
    weight = (groups, 2 * LANES, LANES)
    assert groups == conductors
    scratch = [
        (length.shape, jnp.int32), (link.shape, jnp.int32),
        ((groups, SUBLANES, LANES), jnp.int32), (weight, jnp.bfloat16), (weight, jnp.bfloat16),
    ]
    scratch += [
        (shape, jnp.float32)
        for shape in [
            (4, 2 * conductors, LANES), lines, lines, magnetic.shape, lines, lines, matrix, matrix,
            matrix, rows, (count, 2, LANES), (count, 2, LANES), (count, 1, LANES),
            (count, 1, LANES), edge,
            (2,) + rows, (3,) + end, (3,) + end, (5,) + end, (5,) + end, (5,) + end, (6,) + rows,
            (2,) + end, (2,) + end, (2,) + end, (3,) + end, (6,) + rows,
        ]
    ]
    outs = [
        (cells.shape, jnp.int32), (steer.shape, jnp.float32), (rows, jnp.float32),
        ((3, depth + 1, ny, nz), jnp.float32), (conductivity.shape, jnp.float32),
        (magnetic.shape, jnp.float32), (edge, jnp.float32), (lines, jnp.float32),
        (lines, jnp.float32),
    ]
    semaphores = [depth + 11, 2, 2, 4 * BANDS, 4]
    return pl.pallas_call(
        functools.partial(opening_kernel, mesh_shape),
        out_shape=[pltpu.VMEM(*out) for out in outs],
        in_specs=[hbm] * 11,
        out_specs=[pl.BlockSpec(memory_space=pltpu.VMEM)] * len(outs),
        scratch_shapes=[pltpu.VMEM(*kind) for kind in scratch]
        + [pltpu.SemaphoreType.DMA((number,)) for number in semaphores],
        compiler_params=pltpu.CompilerParams(
            collective_id=0, has_side_effects=True, vmem_limit_bytes=OPENING_VMEM
        ),
        name="lines_and_exchange",
    )(
        *(
            pltpu.with_memory_space_constraint(x, pltpu.HBM)
            for x in (
                cells, steer, electric, magnetic, conductivity, volts, amps, inductance,
                capacitance, length, link,
            )
        )
    )


def whole_base(fresh, old, conductivity, layer, first, hy_before, hz_before):
    rows = pl.ds(first, SUBLANES)
    hx, hy, hz = (fresh[k, layer, rows, :] for k in range(3))
    if first > 0:
        prior = pl.ds(first - 1, SUBLANES)
        dy_hz = hz - fresh[2, layer, prior, :]
        dy_hx = hx - fresh[0, layer, prior, :]
    else:
        dy_hz, dy_hx = behind(hz, 0), behind(hx, 0)
    curls = [
        dy_hz - behind(hy, 1),
        behind(hx, 1) - (hz - hz_before[rows, :]),
        (hy - hy_before[rows, :]) - dy_hx,
    ]
    inverse = 1.0 / (1.0 + conductivity)
    keep = (1.0 - conductivity) * inverse
    factor = COURANT * inverse
    return [keep * e + factor * curl for e, curl in zip(old, curls)], factor


def electric_kernel(
    cell_ref, tangent_ref, induced_ref, field, sigma, fresh, below_ref, volts_ref, amps_ref,
    electric_hbm, magnetic_hbm, volts_hbm, amps_hbm,
    new_ref, word_ref, merged_ref, copy_sem,
):
    _, depth, ny, nz = new_ref.shape
    halves = nz // LANES
    trays = cell_ref.shape[0] // halves
    groups = trays // SUBLANES
    chunks = ny // SUBLANES
    copies = [
        pltpu.make_async_copy(src, dst, copy_sem.at[depth + i])
        for i, (src, dst) in enumerate(
            [(fresh, magnetic_hbm), (amps_ref, amps_hbm), (volts_ref, volts_hbm)]
        )
    ]
    for copy in copies:
        copy.start()
    kept = []
    for half in range(halves):
        where = pl.ds(half, trays, stride=halves)
        cells = cell_ref[where, :]
        weights = [tangent_ref[k, where, :] * induced_ref[where, :] for k in range(3)]
        sums = [jnp.zeros_like(w) for w in weights]
        order = lax.broadcasted_iota(jnp.int32, cells.shape, 0)
        late = jnp.zeros(cells.shape, jnp.int32)
        for tray in range(trays):
            same = cells == cells[tray : tray + 1]
            late = jnp.where(same & (order > tray), 1, late)
            for k in range(3):
                sums[k] = sums[k] + jnp.where(same, weights[k][tray : tray + 1], 0.0)
        for k in range(3):
            merged_ref[k, half] = sums[k]
        block = jnp.where(late == 0, cells >> 3, -1)
        code = jnp.left_shift((order & (SUBLANES - 1)) | SUBLANES, (cells & (SUBLANES - 1)) * 4)
        kept.append((block, code))

    shift = 28 - 4 * lax.broadcasted_iota(jnp.int32, (SUBLANES, LANES), 0)

    def write(layer):
        return pltpu.make_async_copy(
            new_ref.at[:, layer], electric_hbm.at[:, layer], copy_sem.at[layer]
        )

    def one_layer(layer, before=None):
        here = lax.broadcasted_iota(jnp.int32, (chunks, LANES), 0) + layer * chunks
        for half in range(halves):
            block, code = kept[half]
            for group in range(groups):
                word = jnp.zeros((chunks, LANES), jnp.int32)
                for tray in range(group * SUBLANES, (group + 1) * SUBLANES):
                    hit = block[tray : tray + 1] == here
                    word = word | jnp.where(hit, code[tray : tray + 1], 0)
                word_ref[half, group] = word
        for chunk in range(chunks):
            first = chunk * SUBLANES
            rows = pl.ds(first, SUBLANES)
            bases, factor = [field[k, layer, rows, :] for k in range(3)], sigma[layer, rows, :]
            if before is not None:
                bases, factor = whole_base(fresh, bases, factor, layer, first, *before)
            deposits = [[None] * halves for _ in range(3)]
            for half in range(halves):
                picks = []
                for group in range(groups):
                    word = word_ref[half, group, chunk : chunk + 1, :]
                    word = jnp.left_shift(jnp.broadcast_to(word, (SUBLANES, LANES)), shift)
                    low = lax.shift_right_logical(word, 28) & (SUBLANES - 1)
                    picks.append((word < 0, low))
                for k in range(3):
                    deposit = jnp.zeros((SUBLANES, LANES), jnp.float32)
                    for group, (hit, low) in enumerate(picks):
                        part = merged_ref[k, half, group * SUBLANES : (group + 1) * SUBLANES, :]
                        deposit = jnp.where(
                            hit, jnp.take_along_axis(part, low, axis=0), deposit
                        )
                    deposits[k][half] = deposit
            for k in range(3):
                deposit = jnp.concatenate(deposits[k], axis=1)
                new_ref[k, layer, rows, :] = bases[k] - factor * deposit
        write(layer).start()

    def inner(layer, carry):
        one_layer(layer)
        return carry

    lax.fori_loop(1, depth - 1, inner, 0)
    one_layer(0, (below_ref.at[0], below_ref.at[1]))
    one_layer(depth - 1, (fresh.at[1, depth - 2], fresh.at[2, depth - 2]))
    for layer in range(depth):
        write(layer).wait()
    for copy in copies:
        copy.wait()


def field_step(*handed):
    cells, fresh, volts, amps = handed[0], handed[5], handed[7], handed[8]
    _, depth, ny, nz = fresh.shape
    halves = nz // LANES
    trays = cells.shape[0] // halves
    vmem = pl.BlockSpec(memory_space=pltpu.VMEM)
    hbm = pl.BlockSpec(memory_space=pl.ANY)
    shapes = [fresh.shape, fresh.shape, volts.shape, amps.shape]
    return pl.pallas_call(
        electric_kernel,
        out_shape=[jax.ShapeDtypeStruct(shape, jnp.float32) for shape in shapes],
        in_specs=[vmem] * len(handed),
        out_specs=[hbm] * len(shapes),
        scratch_shapes=[
            pltpu.VMEM(fresh.shape, jnp.float32),
            pltpu.VMEM((halves, trays // SUBLANES, ny // SUBLANES, LANES), jnp.int32),
            pltpu.VMEM((3, halves, trays, LANES), jnp.float32),
            pltpu.SemaphoreType.DMA((depth + 3,)),
        ],
        compiler_params=pltpu.CompilerParams(vmem_limit_bytes=CLOSING_VMEM),
        name="field_step",
    )(*handed)


def local(
    mesh_shape,
    electric,
    magnetic,
    conductivity,
    voltage,
    current,
    inverse_inductance,
    inverse_capacitance,
    tangent,
    sample_cell,
    tube_length,
    junction_link,
):
    cells = sample_cell.reshape(-1, LANES)
    steer = tangent.reshape(3, -1, LANES)
    handed = opening(
        mesh_shape, cells, steer, electric, magnetic, conductivity, voltage, current,
        inverse_inductance, inverse_capacitance, tube_length[None, :], junction_link[None, :],
    )
    return tuple(field_step(*handed))


def solution(mesh):
    mesh_shape = (mesh.shape["slab"], mesh.shape["cable"])
    return jax.shard_map(
        functools.partial(local, mesh_shape),
        mesh=mesh,
        in_specs=(
            P(None, AXES, None, None),
            P(None, AXES, None, None),
            P(AXES, None, None),
            P(None, None, AXES),
            P(None, None, AXES),
            P(None, None, AXES),
            P(None, None, AXES),
            P(None, AXES, None),
            P(AXES, None),
            P(AXES),
            P(AXES),
        ),
        out_specs=(
            P(None, AXES, None, None),
            P(None, AXES, None, None),
            P(None, None, AXES),
            P(None, None, AXES),
        ),
        check_vma=False,
    )
```
